32 devices in a mesh: grp: 2 (over x), lat: 8 (over z, y), lon: 2 (over core).
Axes of the slice: x: 2, y: 2, z: 4, core: 2. Of those that a mesh axis runs over, the one named last changes fastest.
Arguments:
- fields: bfloat16 [4, 128, 384, 256], P('grp', 'lat', 'lon'), parts along dimension 0
- mix_gain: float32 [2, 256], replicated, may hold values from 0.1 to 1.9
- lat_weight: bfloat16 [2, 5, 2, 128, 128], replicated, may hold values from -0.25 to 0.25
- lon_weight: bfloat16 [2, 5, 2, 128, 128], replicated, may hold values from -0.25 to 0.25
- mlp_gain: float32 [256], replicated, may hold values from 0.1 to 1.9
- w_in: bfloat16 [256, 1024], replicated, may hold values from -0.375 to 0.375
- w_out: bfloat16 [1024, 256], replicated, may hold values from -0.1875 to 0.1875
- lat_dilation: int32 [2], replicated, may hold values from 1 to 4, as said below
- lon_dilation: int32 [2], replicated, may hold values from 1 to 24, as said below
- ocean: int32 [256, 384], P(('grp', 'lat'), 'lon'), parts along dimension 0, may hold values 0 or 1
Outputs:
- mixed: bfloat16 [4, 128, 384, 256], P('grp', 'lat', 'lon'), parts along dimension 0
The draws below stay inside these ranges and needn't reach their ends.
There are 2 independent parts, one for each index of `grp`. The reference program is written for one: setup_inputs(seed, part) draws one part's arguments, and reference() takes and returns one part's arrays. A program takes and returns all parts, laid end to end along the dimension named above; an argument that names none is the same for every part. Nothing has to cross between parts.
Inputs may be any that keep to these rules, and one draw needn't show every extreme that they name: `lat_dilation`: 4 is taken by exactly one layer in every draw. `lon_dilation`: 24 is taken by exactly one layer in every draw.
All inputs are finite; a program needn't handle non-finite values. No bound on the sum of `ocean` on one device may be relied on, other than what follows from the above.
Results may differ from the reference program's by a relative error of at most 0.0075.
Values may be sent and summed in bfloat16 or wider, within the bound.
A program may use at most 128 MiB of HBM per device.

```python
import math
import jax
import jax.numpy as jnp
from jax import lax

C = 256
F = 1024
GROUPS = 2
CG = 128
TAPS = 5
LAYERS = 2
B = 2
MAXDIL_LAT = 4
MAXDIL_LON = 24
LAT = 128
LON = 384


def draw_fields(key, part):
    shape = (B, LAT, LON, C)
    first, second, third = jax.random.split(key, 3)
    base = jnp.clip(jax.random.normal(first, shape, jnp.float32), -6.0, 6.0)
    cell_scale = jnp.exp(jax.random.uniform(second, (B, LAT, LON, 1), jnp.float32, -0.5 * math.log(10.0), 0.5 * math.log(10.0)))
    chan_scale = jnp.exp(jax.random.uniform(third, (C,), jnp.float32, -0.5 * math.log(10.0), 0.5 * math.log(10.0)))
    return (base * cell_scale * chan_scale * 0.5).astype(jnp.bfloat16)


def dilation_draw(key, largest):
    values = jax.random.randint(key, (LAYERS,), 1, largest)
    chosen = jax.random.randint(jax.random.fold_in(key, 7), (), 0, LAYERS)
    return jnp.where(jnp.arange(LAYERS) == chosen, largest, values).astype(jnp.int32)


def draw_lat_dilation(key, part):
    return dilation_draw(jax.random.fold_in(key, 11), MAXDIL_LAT)


def draw_lon_dilation(key, part):
    return dilation_draw(jax.random.fold_in(key, 13), MAXDIL_LON)


def with_ends(drawn, key, smallest, high):
    dims = drawn.shape
    spot = [jax.random.randint(jax.random.fold_in(key, axis), (), 0, dims[axis]) for axis in range(len(dims))]
    drawn = drawn.at[tuple(spot)].set(smallest)
    longest = dims.index(max(dims))
    spot[longest] = (spot[longest] + 1) % dims[longest]
    return drawn.at[tuple(spot)].set(high)


def normal_values(key, extent, deviation, reach, held_as=jnp.bfloat16):
    return jnp.clip(deviation * jax.random.normal(key, extent, jnp.float32), -reach, reach).astype(held_as)


def setup_inputs(seed: int = 0, part: int = 0) -> dict:
    seeds = jax.random.split(jax.random.key(seed), 11)
    part_splits = jax.random.split(jax.random.fold_in(seeds[10], part), 11)
    return {
        "fields": draw_fields(jax.random.fold_in(jax.random.fold_in(seeds[10], part), 71), part),
        "mix_gain": jnp.clip(1.0 + 0.18 * jax.random.normal(seeds[1], (LAYERS, C), jnp.float32), 0.1, 1.9),
        "lat_weight": normal_values(seeds[2], (LAYERS, TAPS, GROUPS, CG, CG), (TAPS * CG) ** -0.5, 0.25),
        "lon_weight": normal_values(seeds[3], (LAYERS, TAPS, GROUPS, CG, CG), (TAPS * CG) ** -0.5, 0.25),
        "mlp_gain": jnp.clip(1.0 + 0.18 * jax.random.normal(seeds[4], (C,), jnp.float32), 0.1, 1.9),
        "w_in": normal_values(seeds[5], (C, F), C ** -0.5, 0.375),
        "w_out": normal_values(seeds[6], (F, C), F ** -0.5, 0.1875),
        "lat_dilation": draw_lat_dilation(jax.random.fold_in(seeds[10], 71), part),
        "lon_dilation": draw_lon_dilation(jax.random.fold_in(seeds[10], 71), part),
        "ocean": with_ends((jax.random.randint(part_splits[9], (LAT, LON), 0, 3) < 2).astype(jnp.int32), jax.random.fold_in(part_splits[9], 1), 0, 1),
    }


def rms_scale(state, gain):
    wide = state.astype(jnp.float32)
    power = lax.optimization_barrier(jnp.mean(wide * wide, axis=-1, keepdims=True))
    return wide * lax.rsqrt(power + 1e-06) * gain

def grouped(piece, weight):
    shape = piece.shape
    split = piece.reshape(shape[:-1] + (GROUPS, CG)).astype(jnp.float32)
    result = jnp.einsum('blwgc,gcd->blwgd', split, weight.astype(jnp.float32))
    return result.reshape(shape)

def reference(fields, mix_gain, lat_weight, lon_weight, mlp_gain, w_in, w_out, lat_dilation, lon_dilation, ocean):
    half = TAPS // 2
    lat_reach = half * MAXDIL_LAT
    lon_reach = half * MAXDIL_LON
    wet = ocean.astype(jnp.float32)[None, :, :, None]
    state = fields
    for layer in range(LAYERS):
        normed = rms_scale(state, mix_gain[layer]).astype(jnp.bfloat16)
        padded = jnp.pad(normed, ((0, 0), (lat_reach, lat_reach), (0, 0), (0, 0)))
        total = jnp.zeros(normed.shape, jnp.float32)
        for tap in range(TAPS):
            start = (lat_reach + (tap - half) * lat_dilation[layer]).astype(jnp.int32)
            piece = lax.dynamic_slice_in_dim(padded, start, LAT, 1)
            total = total + grouped(piece, lat_weight[layer, tap])
        across = total.astype(jnp.bfloat16)
        wrapped = jnp.concatenate([across[:, :, LON - lon_reach:], across, across[:, :, :lon_reach]], 2)
        total = jnp.zeros(normed.shape, jnp.float32)
        for tap in range(TAPS):
            start = (lon_reach + (tap - half) * lon_dilation[layer]).astype(jnp.int32)
            piece = lax.dynamic_slice_in_dim(wrapped, start, LON, 2)
            total = total + grouped(piece, lon_weight[layer, tap])
        state = (state.astype(jnp.float32) + wet * total).astype(jnp.bfloat16)
    lifted = rms_scale(state, mlp_gain).astype(jnp.bfloat16).reshape(-1, C)
    hidden = jax.nn.silu(jnp.dot(lifted, w_in, preferred_element_type=jnp.float32)).astype(jnp.bfloat16)
    update = jnp.dot(hidden, w_out, preferred_element_type=jnp.float32).reshape(state.shape)
    return (state.astype(jnp.float32) + update).astype(jnp.bfloat16)
```

```python
import functools

import jax
import jax.numpy as jnp
from jax import lax
from jax.experimental import pallas as pl
from jax.experimental.pallas import tpu as pltpu
from jax.sharding import PartitionSpec as P

C = 256
GROUPS = 2
CG = 128
TAPS = 5
HALF = 2
LAYERS = 2
HIDDEN = 1024
REACH = 8
STRIP = 48
BLOCKS = 4
ROWS = BLOCKS * REACH
VMEM_LIMIT = 60 * 1024 * 1024
MESH = pl.DeviceIdType.MESH
bf16 = jnp.bfloat16
f32 = jnp.float32

EDGE, REST, NEAR, FAR, NEAR2, FAR2, BACK0, BACK1 = range(8)


def scaled(wide, gain):
    power = jnp.mean(wide * wide, axis=-1, keepdims=True)
    return wide * lax.rsqrt(power + 1e-06) * gain


def kernel(
    count,
    strips,
    lat_dilation,
    lon_dilation,
    fields,
    ocean,
    mix_gain,
    mlp_gain,
    lat_weight,
    lon_weight,
    w_in,
    w_out,
    out,
    state,
    near,
    far,
    near2,
    far2,
    normed,
    wide1,
    wide2,
    halo_out,
    halo_in,
    raw,
    bank,
    v_in,
    v_out,
    sea,
    pad,
    wet,
    send,
    recv,
    halo_send,
    halo_recv,
    sea_send,
    sea_recv,
    load_sem,
    own_sem,
    keep_sem,
):
    lat = lax.axis_index("lat")
    core = lax.axis_index("lon")
    member = lax.rem(lat, 2)
    other = 1 - member
    partner = {"lat": lat + 1 - 2 * member}
    across_core = {"lon": 1 - core}
    near_to = lat - 2 + 4 * member
    far_to = lat + 2 - 4 * member
    has_near_to = jnp.logical_and(near_to >= 0, near_to < count)
    has_far_to = jnp.logical_and(far_to >= 0, far_to < count)
    near_to = {"lat": near_to}
    far_to = {"lat": far_to}
    wide = (wide1, wide2)

    place = (16 - 8 * member, 24 - 24 * member, 8 + 8 * member, 24 * member)
    near_row = 40 * other
    far_row = 40 * member

    def first_col(k):
        return pl.multiple_of(STRIP * (k + core * (strips - 1 - 2 * k)), STRIP)

    def wide_col(k):
        return pl.multiple_of(STRIP * (1 + k + core * (strips - 1 - 2 * k)), STRIP)

    def halo_col(side):
        turned = side + core * (1 - 2 * side)
        return pl.multiple_of(STRIP * (strips + 1) * turned, STRIP)

    def block(b):
        return pl.ds(b * REACH, REACH)

    def in_hbm(ref, sample, row, k):
        return ref.at[sample, pl.ds(row, REACH), pl.ds(first_col(k), STRIP)]

    def remote(family, k, src, dst, device):
        return pltpu.make_async_remote_copy(
            src_ref=src,
            dst_ref=dst,
            send_sem=send.at[family, k],
            recv_sem=recv.at[family, k],
            device_id=device,
            device_id_type=MESH,
        )

    def edge_copy(k):
        return remote(
            EDGE, k, in_hbm(fields, other, REACH * member, k), state.at[k, block(1)], partner
        )

    def rest_copy(k):
        return remote(
            REST, k, in_hbm(fields, other, REACH * other, k), state.at[k, block(0)], partner
        )

    def near_copy(k):
        return remote(NEAR, k, in_hbm(fields, member, REACH * member, k), near.at[k], near_to)

    def far_copy(k):
        return remote(FAR, k, state.at[k, block(1)], far.at[k], far_to)

    def near2_copy(k):
        rows = pl.ds(REACH + place[3], REACH)
        return remote(NEAR2, k, normed.at[k, rows], near2.at[k], near_to)

    def far2_copy(k):
        rows = pl.ds(REACH + place[1], REACH)
        return remote(FAR2, k, normed.at[k, rows], far2.at[k], far_to)

    def back_copy(b, k):
        row = REACH * (member if b == 0 else other)
        return remote(
            BACK0 + b, k, state.at[k, block(b)], in_hbm(out, member, row, k), partner
        )

    def halo_copy(group, side):
        layer, first, number = ((0, 0, 4), (1, 0, 1), (1, 1, 1), (1, 2, 2))[group]
        rows = pl.ds(first * REACH, number * REACH)
        return pltpu.make_async_remote_copy(
            src_ref=halo_out.at[layer, side, rows],
            dst_ref=halo_in.at[layer, side, rows],
            send_sem=halo_send.at[group, side],
            recv_sem=halo_recv.at[group, side],
            device_id=across_core,
            device_id_type=MESH,
        )

    def sea_copy(b):
        row = REACH * (member if b == 1 else other)
        return pltpu.make_async_remote_copy(
            src_ref=ocean.at[pl.ds(row, REACH)],
            dst_ref=sea.at[b],
            send_sem=sea_send.at[b],
            recv_sem=sea_recv.at[b],
            device_id=partner,
            device_id_type=MESH,
        )

    def own_copy(b, k):
        row = REACH * (other if b == 2 else member)
        return pltpu.make_async_copy(
            in_hbm(fields, member, row, k), state.at[k, block(b)], own_sem.at[b - 2, k]
        )

    def keep_copy(b, k):
        row = REACH * (other if b == 2 else member)
        return pltpu.make_async_copy(
            state.at[k, block(b)], in_hbm(out, member, row, k), keep_sem.at[b - 2, k]
        )

    def sea_own(b):
        row = REACH * (other if b == 2 else member)
        return pltpu.make_async_copy(ocean.at[pl.ds(row, REACH)], sea.at[b], load_sem.at[b + 2])

    loads = (
        pltpu.make_async_copy(lat_weight, raw.at[0], load_sem.at[0]),
        pltpu.make_async_copy(lon_weight, raw.at[1], load_sem.at[1]),
        pltpu.make_async_copy(w_in, v_in, load_sem.at[2]),
        pltpu.make_async_copy(w_out, v_out, load_sem.at[3]),
        sea_own(2),
        sea_own(3),
    )

    barrier = pltpu.get_barrier_semaphore()
    for device, there in (
        (partner, None),
        (across_core, None),
        (near_to, has_near_to),
        (far_to, has_far_to),
    ):
        if there is None:
            pl.semaphore_signal(barrier, inc=1, device_id=device, device_id_type=MESH)
        else:

            @pl.when(there)
            def _():
                pl.semaphore_signal(barrier, inc=1, device_id=device, device_id_type=MESH)

    for copy in loads:
        copy.start()
    pl.semaphore_wait(
        barrier, 2 + has_near_to.astype(jnp.int32) + has_far_to.astype(jnp.int32)
    )

    order = [edge_copy(0)]
    for k in range(strips):
        if k + 1 < strips:
            order.append(edge_copy(k + 1))
        order.append(rest_copy(k))
    for copy in order:
        copy.start()
    for b in (0, 1):
        sea_copy(b).start()

    @pl.when(has_near_to)
    def _():
        for k in range(strips):
            near_copy(k).start()

    for k in range(strips):
        own_copy(2, k).start()
        own_copy(3, k).start()

    bank[...] = jnp.zeros_like(bank)
    loads[0].wait()
    loads[1].wait()
    for which in range(2):
        for layer in range(LAYERS):
            for tap in range(TAPS):
                for g in range(GROUPS):
                    at = tap * C + g * CG
                    bank[which, layer, at : at + CG, g * CG : (g + 1) * CG] = raw[
                        which, layer, tap, g
                    ]
    for copy in loads[2:]:
        copy.wait()
    pad[...] = jnp.zeros_like(pad)
    for b in range(BLOCKS):
        if b < 2:
            sea_copy(b).wait_recv()
        pad[b * REACH : (b + 1) * REACH, 0 : strips * STRIP] = sea[b].astype(f32)
    wet[...] = pad[...].T

    def put(k, row, value, gain):
        normed[k, pl.ds(row, REACH)] = scaled(value.astype(f32), gain).astype(bf16)

    def lat_conv(layer, k, blocks, group):
        dilation = lat_dilation[layer]
        taps = []
        for tap in range(TAPS):
            pieces = []
            for b in blocks:
                start = REACH + place[b] + (tap - HALF) * dilation
                pieces.append(normed[k, pl.ds(start, REACH)].reshape(REACH * STRIP, C))
            taps.append(jnp.concatenate(pieces, 0))
        total = jnp.dot(
            jnp.concatenate(taps, 1), bank[0, layer], preferred_element_type=f32
        )
        number = len(blocks) * REACH
        total = total.astype(bf16).reshape(number, STRIP, C)
        first = blocks[0] * REACH
        spread(layer, first, total, wide_col(k))
        for side, at in ((0, 0), (1, strips - 1)):

            @pl.when(k == at)
            def _():
                halo_out[layer, side, first : first + number] = total
                halo_copy(group, side).start()

    def spread(layer, first, value, col):
        for g in range(GROUPS):
            wide[layer][g, pl.ds(first, value.shape[0]), pl.ds(col, STRIP), :] = value[
                :, :, g * CG : (g + 1) * CG
            ].astype(f32)

    def halo_wait(group, side):
        layer, first, number = ((0, 0, 4), (1, 0, 1), (1, 1, 1), (1, 2, 2))[group]
        halo_copy(group, side).wait_recv()
        rows = slice(first * REACH, (first + number) * REACH)
        spread(layer, first * REACH, halo_in[layer, side, rows], halo_col(side))

    def halo_check(group, k):
        for side, at in ((0, 0), (1, strips - 1)):

            @pl.when(k == at)
            def _():
                halo_wait(group, side)

    def lon_conv(layer, k, first, number):
        dilation = lon_dilation[layer]
        taps = []
        for tap in range(TAPS):
            start = wide_col(k) + (tap - HALF) * dilation
            for g in range(GROUPS):
                piece = wide[layer][g, pl.ds(first, number), pl.ds(start, STRIP), :]
                taps.append(piece.astype(bf16).reshape(number * STRIP, CG))
        total = jnp.dot(
            jnp.concatenate(taps, 1), bank[1, layer], preferred_element_type=f32
        )
        mask = wet[pl.ds(first_col(k), STRIP), :]
        values = []
        for r in range(number):
            old = state[k, first + r].astype(f32)
            part = total[r * STRIP : (r + 1) * STRIP] * mask[:, first + r : first + r + 1]
            values.append((old + part).astype(bf16))
        return values

    def lat_first(k):
        for b in range(BLOCKS):
            put(k, REACH + place[b], state[k, block(b)], mix_gain[0:1])
        for copy, there, ref, row in (
            (near_copy, has_far_to, near, near_row),
            (far_copy, has_near_to, far, far_row),
        ):

            @pl.when(there)
            def _():
                copy(k).wait_recv()
                put(k, row, ref[k], mix_gain[0:1])

            @pl.when(jnp.logical_not(there))
            def _():
                normed[k, pl.ds(row, REACH)] = jnp.zeros((REACH, STRIP, C), bf16)

        lat_conv(0, k, (0, 1, 2, 3), 0)

    def lon_first(k):
        values = lon_conv(0, k, 0, ROWS)
        for b in range(BLOCKS):
            part = jnp.stack(values[b * REACH : (b + 1) * REACH], 0)
            state[k, block(b)] = part
            put(k, REACH + place[b], part, mix_gain[1:2])

        @pl.when(has_near_to)
        def _():
            near2_copy(k).start()

        @pl.when(has_far_to)
        def _():
            far2_copy(k).start()

    def finish(k, first, number):
        new = jnp.concatenate(lon_conv(1, k, first, number), 0).astype(f32)
        lifted = scaled(new, mlp_gain[...]).astype(bf16)
        half = 0.5 * jnp.dot(lifted, v_in[...], preferred_element_type=f32)
        hidden = (half + half * jnp.tanh(half)).astype(bf16)
        update = jnp.dot(hidden, v_out[...], preferred_element_type=f32)
        state[k, first : first + number] = (
            (new + update).astype(bf16).reshape(number, STRIP, C)
        )

    def forward(k):
        edge_copy(k).wait_recv()

        @pl.when(has_far_to)
        def _():
            far_copy(k).start()

    forward(0)

    def step(k, carry):
        @pl.when(k + 1 < strips)
        def _():
            forward(k + 1)

        @pl.when(k < strips)
        def _():
            own_copy(2, k).wait()
            own_copy(3, k).wait()
            rest_copy(k).wait_recv()
            lat_first(k)

        @pl.when(jnp.logical_and(k >= 1, k <= strips))
        def _():
            j = k - 1
            halo_check(0, j)

            @pl.when(has_far_to)
            def _():
                far_copy(j).wait_send()

            lon_first(j)
            lat_conv(1, j, (0,), 1)

        @pl.when(k >= 2)
        def _():
            i = k - 2
            halo_check(1, i)
            finish(i, 0, REACH)
            back_copy(0, i).start()

        return carry

    lax.fori_loop(0, strips + 2, step, 0)

    def halo_rows(copy, there, ref, row, k):
        @pl.when(there)
        def _():
            copy(k).wait_recv()
            normed[k, pl.ds(row, REACH)] = ref[k]

        @pl.when(jnp.logical_not(there))
        def _():
            normed[k, pl.ds(row, REACH)] = jnp.zeros((REACH, STRIP, C), bf16)

    def edge_lat(k, carry):
        halo_rows(near2_copy, has_far_to, near2, near_row, k)
        lat_conv(1, k, (1,), 2)
        return carry

    def keep_lat(k, carry):
        halo_rows(far2_copy, has_near_to, far2, far_row, k)
        lat_conv(1, k, (2, 3), 3)
        return carry

    def edge_finish(k, carry):
        finish(k, REACH, REACH)
        back_copy(1, k).start()
        return carry

    def keep_finish(k, carry):
        finish(k, 2 * REACH, 2 * REACH)
        keep_copy(2, k).start()
        keep_copy(3, k).start()
        return carry

    lax.fori_loop(0, strips, edge_lat, 0)
    lax.fori_loop(0, strips, keep_lat, 0)
    for side in range(2):
        halo_wait(2, side)
    lax.fori_loop(0, strips, edge_finish, 0)
    for side in range(2):
        halo_wait(3, side)
    lax.fori_loop(0, strips, keep_finish, 0)

    for group in range(4):
        for side in range(2):
            halo_copy(group, side).wait_send()
    for b in (0, 1):
        sea_copy(b).wait_send()
    for k in range(strips):
        edge_copy(k).wait_send()
        rest_copy(k).wait_send()

        @pl.when(has_near_to)
        def _():
            near_copy(k).wait_send()
            near2_copy(k).wait_send()

        @pl.when(has_far_to)
        def _():
            far2_copy(k).wait_send()

        keep_copy(2, k).wait()
        keep_copy(3, k).wait()
        back_copy(0, k).wait()
        back_copy(1, k).wait()


def on_device(
    fields,
    mix_gain,
    lat_weight,
    lon_weight,
    mlp_gain,
    w_in,
    w_out,
    lat_dilation,
    lon_dilation,
    ocean,
):
    cols = fields.shape[2]
    strips = cols // STRIP
    count = lax.axis_size("lat")
    width = -(-cols // 128) * 128
    smem = pl.BlockSpec(memory_space=pltpu.SMEM)
    vmem = pl.BlockSpec(memory_space=pltpu.VMEM)
    hbm = pl.BlockSpec(memory_space=pl.ANY)
    held = pltpu.VMEM((strips, ROWS, STRIP, C), bf16)
    halo = pltpu.VMEM((strips, REACH, STRIP, C), bf16)
    wide = pltpu.VMEM((GROUPS, ROWS, cols + 2 * STRIP, CG), f32)
    ends = pltpu.VMEM((LAYERS, 2, ROWS, STRIP, C), bf16)
    dma = pltpu.SemaphoreType.DMA
    cells = 2 * fields.shape[1] * cols
    return pl.pallas_call(
        functools.partial(kernel, count, strips),
        in_specs=[smem, smem, hbm, hbm, vmem, vmem, hbm, hbm, hbm, hbm],
        out_specs=hbm,
        out_shape=jax.ShapeDtypeStruct(fields.shape, bf16),
        scratch_shapes=[
            held,
            halo,
            halo,
            halo,
            halo,
            pltpu.VMEM((strips, ROWS + 2 * REACH, STRIP, C), bf16),
            wide,
            wide,
            ends,
            ends,
            pltpu.VMEM((2, LAYERS, TAPS, GROUPS, CG, CG), bf16),
            pltpu.VMEM((2, LAYERS, TAPS * C, C), bf16),
            pltpu.VMEM((C, HIDDEN), bf16),
            pltpu.VMEM((HIDDEN, C), bf16),
            pltpu.VMEM((BLOCKS, REACH, cols), jnp.int32),
            pltpu.VMEM((128, width), f32),
            pltpu.VMEM((width, 128), f32),
            dma((8, strips)),
            dma((8, strips)),
            dma((4, 2)),
            dma((4, 2)),
            dma((2,)),
            dma((2,)),
            dma((6,)),
            dma((2, strips)),
            dma((2, strips)),
        ],
        compiler_params=pltpu.CompilerParams(
            collective_id=0, has_side_effects=True, vmem_limit_bytes=VMEM_LIMIT
        ),
        cost_estimate=pl.CostEstimate(
            flops=2 * cells * (2 * LAYERS * TAPS * C * C + 2 * C * HIDDEN),
            bytes_accessed=4 * cells * C,
            transcendentals=cells * HIDDEN,
        ),
    )(
        lat_dilation,
        lon_dilation,
        fields,
        ocean,
        mix_gain,
        mlp_gain.reshape(1, C),
        lat_weight,
        lon_weight,
        w_in,
        w_out,
    )


def solution(mesh):
    return jax.shard_map(
        on_device,
        mesh=mesh,
        in_specs=(
            P("grp", "lat", "lon", None),
            P(),
            P(),
            P(),
            P(),
            P(),
            P(),
            P(),
            P(),
            P(("grp", "lat"), "lon"),
        ),
        out_specs=P("grp", "lat", "lon", None),
        check_vma=False,
    )
```

```python
import functools

import jax
import jax.numpy as jnp
from jax import lax
from jax.experimental import pallas as pl
from jax.experimental.pallas import tpu as pltpu
from jax.sharding import PartitionSpec as P

C = 256
GROUPS = 2
CG = 128
TAPS = 5
HALF = 2
LAYERS = 2
HIDDEN = 1024
REACH = 8
STRIP = 48
BLOCKS = 4
ROWS = BLOCKS * REACH
VMEM_LIMIT = 60 * 1024 * 1024
MESH = pl.DeviceIdType.MESH
bf16 = jnp.bfloat16
f32 = jnp.float32

EDGE, REST, NEAR, FAR, NEAR2, FAR2, BACK0, BACK1 = range(8)


def scaled(wide, gain):
    power = jnp.mean(wide * wide, axis=-1, keepdims=True)
    return wide * lax.rsqrt(power + 1e-06) * gain


def kernel(
    count,
    strips,
    lat_dilation,
    lon_dilation,
    fields,
    ocean,
    mix_gain,
    mlp_gain,
    lat_weight,
    lon_weight,
    w_in,
    w_out,
    out,
    state,
    near,
    far,
    near2,
    far2,
    normed,
    wide1,
    wide2,
    halo_out,
    halo_in,
    raw,
    bank,
    v_in,
    v_out,
    sea,
    pad,
    wet,
    send,
    recv,
    halo_send,
    halo_recv,
    sea_send,
    sea_recv,
    load_sem,
    own_sem,
    keep_sem,
):
    lat = lax.axis_index("lat")
    core = lax.axis_index("lon")
    member = lax.rem(lat, 2)
    other = 1 - member
    partner = {"lat": lat + 1 - 2 * member}
    across_core = {"lon": 1 - core}
    near_to = lat - 2 + 4 * member
    far_to = lat + 2 - 4 * member
    has_near_to = jnp.logical_and(near_to >= 0, near_to < count)
    has_far_to = jnp.logical_and(far_to >= 0, far_to < count)
    near_to = {"lat": near_to}
    far_to = {"lat": far_to}
    wide = (wide1, wide2)

    place = (16 - 8 * member, 24 - 24 * member, 8 + 8 * member, 24 * member)
    near_row = 40 * other
    far_row = 40 * member

    def first_col(k):
        return pl.multiple_of(STRIP * (k + core * (strips - 1 - 2 * k)), STRIP)

    def wide_col(k):
        return pl.multiple_of(STRIP * (1 + k + core * (strips - 1 - 2 * k)), STRIP)

    def halo_col(side):
        turned = side + core * (1 - 2 * side)
        return pl.multiple_of(STRIP * (strips + 1) * turned, STRIP)

    def block(b):
        return pl.ds(b * REACH, REACH)

    def in_hbm(ref, sample, row, k):
        return ref.at[sample, pl.ds(row, REACH), pl.ds(first_col(k), STRIP)]

    def remote(family, k, src, dst, device):
        return pltpu.make_async_remote_copy(
            src_ref=src,
            dst_ref=dst,
            send_sem=send.at[family, k],
            recv_sem=recv.at[family, k],
            device_id=device,
            device_id_type=MESH,
        )

    def edge_copy(k):
        return remote(
            EDGE, k, in_hbm(fields, other, REACH * member, k), state.at[k, block(1)], partner
        )

    def rest_copy(k):
        return remote(
            REST, k, in_hbm(fields, other, REACH * other, k), state.at[k, block(0)], partner
        )

    def near_copy(k):
        return remote(NEAR, k, in_hbm(fields, member, REACH * member, k), near.at[k], near_to)

    def far_copy(k):
        return remote(FAR, k, state.at[k, block(1)], far.at[k], far_to)

    def near2_copy(k):
        rows = pl.ds(REACH + place[3], REACH)
        return remote(NEAR2, k, normed.at[k, rows], near2.at[k], near_to)

    def far2_copy(k):
        rows = pl.ds(REACH + place[1], REACH)
        return remote(FAR2, k, normed.at[k, rows], far2.at[k], far_to)

    def back_copy(b, k):
        row = REACH * (member if b == 0 else other)
        return remote(
            BACK0 + b, k, state.at[k, block(b)], in_hbm(out, member, row, k), partner
        )

    def halo_copy(group, side):
        layer, first, number = ((0, 0, 4), (1, 0, 1), (1, 1, 1), (1, 2, 2))[group]
        rows = pl.ds(first * REACH, number * REACH)
        return pltpu.make_async_remote_copy(
            src_ref=halo_out.at[layer, side, rows],
            dst_ref=halo_in.at[layer, side, rows],
            send_sem=halo_send.at[group, side],
            recv_sem=halo_recv.at[group, side],
            device_id=across_core,
            device_id_type=MESH,
        )

    def sea_copy(b):
        row = REACH * (member if b == 1 else other)
        return pltpu.make_async_remote_copy(
            src_ref=ocean.at[pl.ds(row, REACH)],
            dst_ref=sea.at[b],
            send_sem=sea_send.at[b],
            recv_sem=sea_recv.at[b],
            device_id=partner,
            device_id_type=MESH,
        )

    def own_copy(b, k):
        row = REACH * (other if b == 2 else member)
        return pltpu.make_async_copy(
            in_hbm(fields, member, row, k), state.at[k, block(b)], own_sem.at[b - 2, k]
        )

    def keep_copy(b, k):
        row = REACH * (other if b == 2 else member)
        return pltpu.make_async_copy(
            state.at[k, block(b)], in_hbm(out, member, row, k), keep_sem.at[b - 2, k]
        )

    def sea_own(b):
        row = REACH * (other if b == 2 else member)
        return pltpu.make_async_copy(ocean.at[pl.ds(row, REACH)], sea.at[b], load_sem.at[b + 2])

    loads = (
        pltpu.make_async_copy(lat_weight, raw.at[0], load_sem.at[0]),
        pltpu.make_async_copy(lon_weight, raw.at[1], load_sem.at[1]),
        pltpu.make_async_copy(w_in, v_in, load_sem.at[2]),
        pltpu.make_async_copy(w_out, v_out, load_sem.at[3]),
        sea_own(2),
        sea_own(3),
    )

    barrier = pltpu.get_barrier_semaphore()
    for device, there in (
        (partner, None),
        (across_core, None),
        (near_to, has_near_to),
        (far_to, has_far_to),
    ):
        if there is None:
            pl.semaphore_signal(barrier, inc=1, device_id=device, device_id_type=MESH)
        else:

            @pl.when(there)
            def _():
                pl.semaphore_signal(barrier, inc=1, device_id=device, device_id_type=MESH)

    for copy in loads:
        copy.start()
    pl.semaphore_wait(
        barrier, 2 + has_near_to.astype(jnp.int32) + has_far_to.astype(jnp.int32)
    )

    for b in (0, 1):
        sea_copy(b).start()
    order = [edge_copy(0)]
    for k in range(strips):
        if k + 1 < strips:
            order.append(edge_copy(k + 1))
        order.append(rest_copy(k))
    for copy in order:
        copy.start()
    @pl.when(has_near_to)
    def _():
        for k in range(strips):
            near_copy(k).start()

    for k in range(strips):
        own_copy(2, k).start()
        own_copy(3, k).start()

    bank[...] = jnp.zeros_like(bank)
    loads[0].wait()
    loads[1].wait()
    for which in range(2):
        for layer in range(LAYERS):
            for tap in range(TAPS):
                for g in range(GROUPS):
                    at = tap * C + g * CG
                    bank[which, layer, at : at + CG, g * CG : (g + 1) * CG] = raw[
                        which, layer, tap, g
                    ]
    for copy in loads[2:]:
        copy.wait()
    pad[...] = jnp.zeros_like(pad)
    for b in range(BLOCKS):
        if b < 2:
            sea_copy(b).wait_recv()
        pad[b * REACH : (b + 1) * REACH, 0 : strips * STRIP] = sea[b].astype(f32)
    wet[...] = pad[...].T

    def put(k, row, value, gain):
        normed[k, pl.ds(row, REACH)] = scaled(value.astype(f32), gain).astype(bf16)

    def lat_conv(layer, k, blocks, group):
        dilation = lat_dilation[layer]
        taps = []
        for tap in range(TAPS):
            pieces = []
            for b in blocks:
                start = REACH + place[b] + (tap - HALF) * dilation
                pieces.append(normed[k, pl.ds(start, REACH)].reshape(REACH * STRIP, C))
            taps.append(jnp.concatenate(pieces, 0))
        total = jnp.dot(
            jnp.concatenate(taps, 1), bank[0, layer], preferred_element_type=f32
        )
        number = len(blocks) * REACH
        total = total.astype(bf16).reshape(number, STRIP, C)
        first = blocks[0] * REACH
        spread(layer, first, total, wide_col(k))
        for side, at in ((0, 0), (1, strips - 1)):

            @pl.when(k == at)
            def _():
                halo_out[layer, side, first : first + number] = total
                halo_copy(group, side).start()

    def spread(layer, first, value, col):
        for g in range(GROUPS):
            wide[layer][g, pl.ds(first, value.shape[0]), pl.ds(col, STRIP), :] = value[
                :, :, g * CG : (g + 1) * CG
            ].astype(f32)

    def halo_wait(group, side):
        layer, first, number = ((0, 0, 4), (1, 0, 1), (1, 1, 1), (1, 2, 2))[group]
        halo_copy(group, side).wait_recv()
        rows = slice(first * REACH, (first + number) * REACH)
        spread(layer, first * REACH, halo_in[layer, side, rows], halo_col(side))

    def halo_check(group, k):
        for side, at in ((0, 0), (1, strips - 1)):

            @pl.when(k == at)
            def _():
                halo_wait(group, side)

    def lon_conv(layer, k, first, number):
        dilation = lon_dilation[layer]
        taps = []
        for tap in range(TAPS):
            start = wide_col(k) + (tap - HALF) * dilation
            for g in range(GROUPS):
                piece = wide[layer][g, pl.ds(first, number), pl.ds(start, STRIP), :]
                taps.append(piece.astype(bf16).reshape(number * STRIP, CG))
        total = jnp.dot(
            jnp.concatenate(taps, 1), bank[1, layer], preferred_element_type=f32
        )
        mask = wet[pl.ds(first_col(k), STRIP), :]
        values = []
        for r in range(number):
            old = state[k, first + r].astype(f32)
            part = total[r * STRIP : (r + 1) * STRIP] * mask[:, first + r : first + r + 1]
            values.append((old + part).astype(bf16))
        return values

    def lat_first(k):
        for b in range(BLOCKS):
            put(k, REACH + place[b], state[k, block(b)], mix_gain[0:1])
        for copy, there, ref, row in (
            (near_copy, has_far_to, near, near_row),
            (far_copy, has_near_to, far, far_row),
        ):

            @pl.when(there)
            def _():
                copy(k).wait_recv()
                put(k, row, ref[k], mix_gain[0:1])

            @pl.when(jnp.logical_not(there))
            def _():
                normed[k, pl.ds(row, REACH)] = jnp.zeros((REACH, STRIP, C), bf16)

        lat_conv(0, k, (0, 1, 2, 3), 0)

    def lon_first(k):
        values = lon_conv(0, k, 0, ROWS)
        for b in range(BLOCKS):
            part = jnp.stack(values[b * REACH : (b + 1) * REACH], 0)
            state[k, block(b)] = part
            put(k, REACH + place[b], part, mix_gain[1:2])

        @pl.when(has_near_to)
        def _():
            near2_copy(k).start()

        @pl.when(has_far_to)
        def _():
            far2_copy(k).start()

    def finish(k, first, number):
        new = jnp.concatenate(lon_conv(1, k, first, number), 0).astype(f32)
        lifted = scaled(new, mlp_gain[...]).astype(bf16)
        half = 0.5 * jnp.dot(lifted, v_in[...], preferred_element_type=f32)
        hidden = (half + half * jnp.tanh(half)).astype(bf16)
        update = jnp.dot(hidden, v_out[...], preferred_element_type=f32)
        state[k, first : first + number] = (
            (new + update).astype(bf16).reshape(number, STRIP, C)
        )

    def forward(k):
        edge_copy(k).wait_recv()

        @pl.when(has_far_to)
        def _():
            far_copy(k).start()

    forward(0)

    def step(k, carry):
        @pl.when(k + 1 < strips)
        def _():
            forward(k + 1)

        @pl.when(k < strips)
        def _():
            own_copy(2, k).wait()
            own_copy(3, k).wait()
            rest_copy(k).wait_recv()
            lat_first(k)

        @pl.when(jnp.logical_and(k >= 1, k <= strips))
        def _():
            j = k - 1
            halo_check(0, j)

            @pl.when(has_far_to)
            def _():
                far_copy(j).wait_send()

            lon_first(j)
            lat_conv(1, j, (0,), 1)

        @pl.when(k >= 2)
        def _():
            i = k - 2
            halo_check(1, i)
            finish(i, 0, REACH)
            back_copy(0, i).start()

        return carry

    lax.fori_loop(0, strips + 2, step, 0)

    def halo_rows(copy, there, ref, row, k):
        @pl.when(there)
        def _():
            copy(k).wait_recv()
            normed[k, pl.ds(row, REACH)] = ref[k]

        @pl.when(jnp.logical_not(there))
        def _():
            normed[k, pl.ds(row, REACH)] = jnp.zeros((REACH, STRIP, C), bf16)

    def edge_lat(k, carry):
        halo_rows(near2_copy, has_far_to, near2, near_row, k)
        lat_conv(1, k, (1,), 2)
        return carry

    def keep_lat(k, carry):
        halo_rows(far2_copy, has_near_to, far2, far_row, k)
        lat_conv(1, k, (2, 3), 3)
        return carry

    def edge_finish(k, carry):
        finish(k, REACH, REACH)
        back_copy(1, k).start()
        return carry

    def keep_finish(k, carry):
        finish(k, 2 * REACH, 2 * REACH)
        keep_copy(2, k).start()
        keep_copy(3, k).start()
        return carry

    lax.fori_loop(0, strips, edge_lat, 0)
    lax.fori_loop(0, strips, keep_lat, 0)
    for side in range(2):
        halo_wait(2, side)
    lax.fori_loop(0, strips, edge_finish, 0)
    for side in range(2):
        halo_wait(3, side)
    lax.fori_loop(0, strips, keep_finish, 0)

    for group in range(4):
        for side in range(2):
            halo_copy(group, side).wait_send()
    for b in (0, 1):
        sea_copy(b).wait_send()
    for k in range(strips):
        edge_copy(k).wait_send()
        rest_copy(k).wait_send()

        @pl.when(has_near_to)
        def _():
            near_copy(k).wait_send()
            near2_copy(k).wait_send()

        @pl.when(has_far_to)
        def _():
            far2_copy(k).wait_send()

        keep_copy(2, k).wait()
        keep_copy(3, k).wait()
        back_copy(0, k).wait()
        back_copy(1, k).wait()


def on_device(
    fields,
    mix_gain,
    lat_weight,
    lon_weight,
    mlp_gain,
    w_in,
    w_out,
    lat_dilation,
    lon_dilation,
    ocean,
):
    cols = fields.shape[2]
    strips = cols // STRIP
    count = lax.axis_size("lat")
    width = -(-cols // 128) * 128
    smem = pl.BlockSpec(memory_space=pltpu.SMEM)
    vmem = pl.BlockSpec(memory_space=pltpu.VMEM)
    hbm = pl.BlockSpec(memory_space=pl.ANY)
    held = pltpu.VMEM((strips, ROWS, STRIP, C), bf16)
    halo = pltpu.VMEM((strips, REACH, STRIP, C), bf16)
    wide = pltpu.VMEM((GROUPS, ROWS, cols + 2 * STRIP, CG), f32)
    ends = pltpu.VMEM((LAYERS, 2, ROWS, STRIP, C), bf16)
    dma = pltpu.SemaphoreType.DMA
    cells = 2 * fields.shape[1] * cols
    return pl.pallas_call(
        functools.partial(kernel, count, strips),
        in_specs=[smem, smem, hbm, hbm, vmem, vmem, hbm, hbm, hbm, hbm],
        out_specs=hbm,
        out_shape=jax.ShapeDtypeStruct(fields.shape, bf16),
        scratch_shapes=[
            held,
            halo,
            halo,
            halo,
            halo,
            pltpu.VMEM((strips, ROWS + 2 * REACH, STRIP, C), bf16),
            wide,
            wide,
            ends,
            ends,
            pltpu.VMEM((2, LAYERS, TAPS, GROUPS, CG, CG), bf16),
            pltpu.VMEM((2, LAYERS, TAPS * C, C), bf16),
            pltpu.VMEM((C, HIDDEN), bf16),
            pltpu.VMEM((HIDDEN, C), bf16),
            pltpu.VMEM((BLOCKS, REACH, cols), jnp.int32),
            pltpu.VMEM((128, width), f32),
            pltpu.VMEM((width, 128), f32),
            dma((8, strips)),
            dma((8, strips)),
            dma((4, 2)),
            dma((4, 2)),
            dma((2,)),
            dma((2,)),
            dma((6,)),
            dma((2, strips)),
            dma((2, strips)),
        ],
        compiler_params=pltpu.CompilerParams(
            collective_id=0, has_side_effects=True, vmem_limit_bytes=VMEM_LIMIT
        ),
        cost_estimate=pl.CostEstimate(
            flops=2 * cells * (2 * LAYERS * TAPS * C * C + 2 * C * HIDDEN),
            bytes_accessed=4 * cells * C,
            transcendentals=cells * HIDDEN,
        ),
    )(
        lat_dilation,
        lon_dilation,
        fields,
        ocean,
        mix_gain,
        mlp_gain.reshape(1, C),
        lat_weight,
        lon_weight,
        w_in,
        w_out,
    )


def solution(mesh):
    return jax.shard_map(
        on_device,
        mesh=mesh,
        in_specs=(
            P("grp", "lat", "lon", None),
            P(),
            P(),
            P(),
            P(),
            P(),
            P(),
            P(),
            P(),
            P(("grp", "lat"), "lon"),
        ),
        out_specs=P("grp", "lat", "lon", None),
        check_vma=False,
    )
```

```python
import functools

import jax
import jax.numpy as jnp
from jax import lax
from jax.experimental import pallas as pl
from jax.experimental.pallas import tpu as pltpu
from jax.sharding import PartitionSpec as P

C = 256
GROUPS = 2
CG = 128
TAPS = 5
HALF = 2
LAYERS = 2
HIDDEN = 1024
REACH = 8
STRIP = 48
BLOCKS = 4
GROUPED = ((0, 0, 3), (0, 3, 1), (1, 0, 1), (1, 1, 1), (1, 2, 2))
ROWS = BLOCKS * REACH
VMEM_LIMIT = 60 * 1024 * 1024
MESH = pl.DeviceIdType.MESH
bf16 = jnp.bfloat16
f32 = jnp.float32

EDGE, REST, NEAR, FAR, NEAR2, FAR2, BACK0, BACK1 = range(8)


def scaled(wide, gain):
    power = jnp.mean(wide * wide, axis=-1, keepdims=True)
    return wide * lax.rsqrt(power + 1e-06) * gain


def kernel(
    count,
    strips,
    lat_dilation_in,
    lon_dilation_in,
    fields,
    ocean,
    mix_gain_in,
    mlp_gain_in,
    lat_weight,
    lon_weight,
    w_in,
    w_out,
    out,
    state,
    near,
    far,
    near2,
    far2,
    normed,
    wide1,
    wide2,
    halo_out,
    halo_in,
    raw,
    bank,
    v_in,
    v_out,
    sea,
    pad,
    wet,
    lat_dilation,
    lon_dilation,
    mix_gain,
    mlp_gain,
    send,
    recv,
    halo_send,
    halo_recv,
    sea_send,
    sea_recv,
    load_sem,
    own_sem,
    keep_sem,
):
    lat = lax.axis_index("lat")
    core = lax.axis_index("lon")
    member = lax.rem(lat, 2)
    other = 1 - member
    partner = {"lat": lat + 1 - 2 * member}
    across_core = {"lon": 1 - core}
    near_to = lat - 2 + 4 * member
    far_to = lat + 2 - 4 * member
    has_near_to = jnp.logical_and(near_to >= 0, near_to < count)
    has_far_to = jnp.logical_and(far_to >= 0, far_to < count)
    near_to = {"lat": near_to}
    far_to = {"lat": far_to}
    wide = (wide1, wide2)

    place = (16 - 8 * member, 24 - 24 * member, 8 + 8 * member, 24 * member)
    near_row = 40 * other
    far_row = 40 * member

    def first_col(k):
        return pl.multiple_of(STRIP * (k + core * (strips - 1 - 2 * k)), STRIP)

    def wide_col(k):
        return pl.multiple_of(STRIP * (1 + k + core * (strips - 1 - 2 * k)), STRIP)

    def halo_col(side):
        turned = side + core * (1 - 2 * side)
        return pl.multiple_of(STRIP * (strips + 1) * turned, STRIP)

    def block(b):
        return pl.ds(b * REACH, REACH)

    def part_of(ref, sample, row, k):
        return ref.at[sample, pl.ds(row, REACH), pl.ds(first_col(k), STRIP)]

    def remote(family, k, src, dst, device):
        return pltpu.make_async_remote_copy(
            src_ref=src,
            dst_ref=dst,
            send_sem=send.at[family, k],
            recv_sem=recv.at[family, k],
            device_id=device,
            device_id_type=MESH,
        )

    def edge_copy(k):
        return remote(
            EDGE, k, part_of(fields, other, REACH * member, k), state.at[k, block(1)], partner
        )

    def rest_copy(k):
        return remote(
            REST, k, part_of(fields, other, REACH * other, k), state.at[k, block(0)], partner
        )

    def near_copy(k):
        return remote(NEAR, k, part_of(fields, member, REACH * member, k), near.at[k], near_to)

    def far_copy(k):
        return remote(FAR, k, state.at[k, block(1)], far.at[k], far_to)

    def near2_copy(k):
        rows = pl.ds(REACH + place[3], REACH)
        return remote(NEAR2, k, normed.at[k, rows], near2.at[k], near_to)

    def far2_copy(k):
        rows = pl.ds(REACH + place[1], REACH)
        return remote(FAR2, k, normed.at[k, rows], far2.at[k], far_to)

    def back_copy(b, k):
        row = REACH * (member if b == 0 else other)
        return remote(
            BACK0 + b, k, state.at[k, block(b)], part_of(out, member, row, k), partner
        )

    def halo_copy(group, side):
        layer, first, number = GROUPED[group]
        rows = pl.ds(first * REACH, number * REACH)
        return pltpu.make_async_remote_copy(
            src_ref=halo_out.at[layer, side, rows],
            dst_ref=halo_in.at[layer, side, rows],
            send_sem=halo_send.at[group, side],
            recv_sem=halo_recv.at[group, side],
            device_id=across_core,
            device_id_type=MESH,
        )

    def sea_copy(b):
        row = REACH * (member if b == 1 else other)
        return pltpu.make_async_remote_copy(
            src_ref=ocean.at[pl.ds(row, REACH)],
            dst_ref=sea.at[b],
            send_sem=sea_send.at[b],
            recv_sem=sea_recv.at[b],
            device_id=partner,
            device_id_type=MESH,
        )

    def own_copy(b, k):
        row = REACH * (other if b == 2 else member)
        return pltpu.make_async_copy(
            part_of(fields, member, row, k), state.at[k, block(b)], own_sem.at[b - 2, k]
        )

    def keep_copy(b, k):
        row = REACH * (other if b == 2 else member)
        return pltpu.make_async_copy(
            state.at[k, block(b)], part_of(out, member, row, k), keep_sem.at[b - 2, k]
        )

    def sea_own(b):
        row = REACH * (other if b == 2 else member)
        return pltpu.make_async_copy(ocean.at[pl.ds(row, REACH)], sea.at[b], load_sem.at[b + 2])

    loads = (
        pltpu.make_async_copy(lat_weight, raw.at[0], load_sem.at[0]),
        pltpu.make_async_copy(lon_weight, raw.at[1], load_sem.at[1]),
        pltpu.make_async_copy(w_in, v_in, load_sem.at[2]),
        pltpu.make_async_copy(w_out, v_out, load_sem.at[3]),
        sea_own(2),
        sea_own(3),
        pltpu.make_async_copy(lat_dilation_in, lat_dilation, load_sem.at[6]),
        pltpu.make_async_copy(lon_dilation_in, lon_dilation, load_sem.at[7]),
        pltpu.make_async_copy(mix_gain_in, mix_gain, load_sem.at[8]),
        pltpu.make_async_copy(mlp_gain_in, mlp_gain, load_sem.at[9]),
    )

    barrier = pltpu.get_barrier_semaphore()
    for device, there in (
        (partner, None),
        (across_core, None),
        (near_to, has_near_to),
        (far_to, has_far_to),
    ):
        if there is None:
            pl.semaphore_signal(barrier, inc=1, device_id=device, device_id_type=MESH)
        else:

            @pl.when(there)
            def _():
                pl.semaphore_signal(barrier, inc=1, device_id=device, device_id_type=MESH)

    for copy in loads:
        copy.start()
    pl.semaphore_wait(
        barrier, 2 + has_near_to.astype(jnp.int32) + has_far_to.astype(jnp.int32)
    )

    for b in (0, 1):
        sea_copy(b).start()
    order = [edge_copy(0)]
    for k in range(strips):
        if k + 1 < strips:
            order.append(edge_copy(k + 1))
        order.append(rest_copy(k))
    for copy in order:
        copy.start()
    @pl.when(has_near_to)
    def _():
        for k in range(strips):
            near_copy(k).start()

    for k in range(strips):
        own_copy(2, k).start()
        own_copy(3, k).start()

    bank[...] = jnp.zeros_like(bank)
    loads[0].wait()
    loads[1].wait()
    for which in range(2):
        for layer in range(LAYERS):
            for tap in range(TAPS):
                for g in range(GROUPS):
                    at = tap * C + g * CG
                    bank[which, layer, at : at + CG, g * CG : (g + 1) * CG] = raw[
                        which, layer, tap, g
                    ]
    for copy in loads[2:]:
        copy.wait()
    pad[...] = jnp.zeros_like(pad)
    for b in range(BLOCKS):
        if b < 2:
            sea_copy(b).wait_recv()
        pad[b * REACH : (b + 1) * REACH, 0 : strips * STRIP] = sea[b].astype(f32)
    wet[...] = pad[...].T

    def put(k, row, value, gain):
        normed[k, pl.ds(row, REACH)] = scaled(value.astype(f32), gain).astype(bf16)

    def lat_conv(k, group):
        layer, first, number = GROUPED[group]
        blocks = range(first, first + number)
        number *= REACH
        first *= REACH
        dilation = lat_dilation[layer]
        taps = []
        for tap in range(TAPS):
            pieces = []
            for b in blocks:
                start = REACH + place[b] + (tap - HALF) * dilation
                pieces.append(normed[k, pl.ds(start, REACH)].reshape(REACH * STRIP, C))
            taps.append(jnp.concatenate(pieces, 0))
        total = jnp.dot(
            jnp.concatenate(taps, 1), bank[0, layer], preferred_element_type=f32
        )
        total = total.astype(bf16).reshape(number, STRIP, C)
        spread(layer, first, total, wide_col(k))
        for side, at in ((0, 0), (1, strips - 1)):

            @pl.when(k == at)
            def _():
                halo_out[layer, side, first : first + number] = total
                halo_copy(group, side).start()

    def spread(layer, first, value, col):
        for g in range(GROUPS):
            wide[layer][g, pl.ds(first, value.shape[0]), pl.ds(col, STRIP), :] = value[
                :, :, g * CG : (g + 1) * CG
            ].astype(f32)

    def halo_wait(group, side):
        layer, first, number = GROUPED[group]
        halo_copy(group, side).wait_recv()
        rows = slice(first * REACH, (first + number) * REACH)
        spread(layer, first * REACH, halo_in[layer, side, rows], halo_col(side))

    def halo_check(group, k):
        for side, at in ((0, 0), (1, strips - 1)):

            @pl.when(k == at)
            def _():
                halo_wait(group, side)

    def lon_conv(layer, k, first, number):
        dilation = lon_dilation[layer]
        taps = []
        for tap in range(TAPS):
            start = wide_col(k) + (tap - HALF) * dilation
            for g in range(GROUPS):
                piece = wide[layer][g, pl.ds(first, number), pl.ds(start, STRIP), :]
                taps.append(piece.astype(bf16).reshape(number * STRIP, CG))
        total = jnp.dot(
            jnp.concatenate(taps, 1), bank[1, layer], preferred_element_type=f32
        )
        mask = wet[pl.ds(first_col(k), STRIP), :]
        values = []
        for r in range(number):
            old = state[k, first + r].astype(f32)
            part = total[r * STRIP : (r + 1) * STRIP] * mask[:, first + r : first + r + 1]
            values.append((old + part).astype(bf16))
        return values

    def early(k):
        edge_copy(k).wait_recv()

        @pl.when(has_far_to)
        def _():
            far_copy(k).start()

        own_copy(2, k).wait()
        own_copy(3, k).wait()
        for b in (1, 2, 3):
            put(k, REACH + place[b], state[k, block(b)], mix_gain[0:1])
        raw_rows(near_copy, has_far_to, near, near_row, k)

    def raw_rows(copy, there, ref, row, k):
        @pl.when(there)
        def _():
            copy(k).wait_recv()
            put(k, row, ref[k], mix_gain[0:1])

        @pl.when(jnp.logical_not(there))
        def _():
            normed[k, pl.ds(row, REACH)] = jnp.zeros((REACH, STRIP, C), bf16)

    def outer_lat(k):
        raw_rows(far_copy, has_near_to, far, far_row, k)
        lat_conv(k, 1)

    def lon_first(k, first, number):
        values = lon_conv(0, k, first * REACH, number * REACH)
        for at in range(number):
            b = first + at
            part = jnp.stack(values[at * REACH : (at + 1) * REACH], 0)
            state[k, block(b)] = part
            put(k, REACH + place[b], part, mix_gain[1:2])

    def outer_lon(k):
        halo_check(1, k)
        lon_first(k, 3, 1)

        @pl.when(has_near_to)
        def _():
            near2_copy(k).start()

    def finish(k, first, number):
        new = jnp.concatenate(lon_conv(1, k, first, number), 0).astype(f32)
        lifted = scaled(new, mlp_gain[...]).astype(bf16)
        half = 0.5 * jnp.dot(lifted, v_in[...], preferred_element_type=f32)
        hidden = (half + half * jnp.tanh(half)).astype(bf16)
        update = jnp.dot(hidden, v_out[...], preferred_element_type=f32)
        state[k, first : first + number] = (
            (new + update).astype(bf16).reshape(number, STRIP, C)
        )

    early(0)

    def step(k, carry):
        @pl.when(k + 1 < strips)
        def _():
            early(k + 1)
            outer_lat(k)

        @pl.when(jnp.logical_and(k >= 1, k + 1 < strips))
        def _():
            outer_lon(k - 1)

        @pl.when(k < strips)
        def _():
            rest_copy(k).wait_recv()
            put(k, REACH + place[0], state[k, block(0)], mix_gain[0:1])
            lat_conv(k, 0)

        @pl.when(jnp.logical_and(k >= 1, k <= strips))
        def _():
            j = k - 1
            halo_check(0, j)

            @pl.when(has_far_to)
            def _():
                far_copy(j).wait_send()

            lon_first(j, 0, 3)

            @pl.when(has_far_to)
            def _():
                far2_copy(j).start()

            lat_conv(j, 2)

        @pl.when(k >= 2)
        def _():
            i = k - 2
            halo_check(2, i)
            finish(i, 0, REACH)
            back_copy(0, i).start()

        @pl.when(k == strips - 1)
        def _():
            outer_lat(k)

        @pl.when(k >= strips)
        def _():
            outer_lon(k - 2)

        return carry

    lax.fori_loop(0, strips + 2, step, 0)

    def halo_rows(copy, there, ref, row, k):
        @pl.when(there)
        def _():
            copy(k).wait_recv()
            normed[k, pl.ds(row, REACH)] = ref[k]

        @pl.when(jnp.logical_not(there))
        def _():
            normed[k, pl.ds(row, REACH)] = jnp.zeros((REACH, STRIP, C), bf16)

    def edge_step(k, carry):
        @pl.when(k < strips)
        def _():
            halo_rows(near2_copy, has_far_to, near2, near_row, k)
            lat_conv(k, 3)

        @pl.when(k >= 1)
        def _():
            halo_check(3, k - 1)
            finish(k - 1, REACH, REACH)
            back_copy(1, k - 1).start()

        @pl.when(k < strips)
        def _():
            halo_rows(far2_copy, has_near_to, far2, far_row, k)
            lat_conv(k, 4)

        return carry

    def keep_step(k, carry):
        halo_check(4, k)
        finish(k, 2 * REACH, 2 * REACH)
        keep_copy(2, k).start()
        keep_copy(3, k).start()
        return carry

    lax.fori_loop(0, strips + 1, edge_step, 0)
    lax.fori_loop(0, strips, keep_step, 0)

    for group in range(len(GROUPED)):
        for side in range(2):
            halo_copy(group, side).wait_send()
    for b in (0, 1):
        sea_copy(b).wait_send()
    for k in range(strips):
        edge_copy(k).wait_send()
        rest_copy(k).wait_send()

        @pl.when(has_near_to)
        def _():
            near_copy(k).wait_send()
            near2_copy(k).wait_send()

        @pl.when(has_far_to)
        def _():
            far2_copy(k).wait_send()

        keep_copy(2, k).wait()
        keep_copy(3, k).wait()
        back_copy(0, k).wait()
        back_copy(1, k).wait()


def on_device(
    fields,
    mix_gain,
    lat_weight,
    lon_weight,
    mlp_gain,
    w_in,
    w_out,
    lat_dilation,
    lon_dilation,
    ocean,
):
    cols = fields.shape[2]
    strips = cols // STRIP
    count = lax.axis_size("lat")
    width = -(-cols // 128) * 128
    vmem = pl.BlockSpec(memory_space=pltpu.VMEM)
    hbm = pl.BlockSpec(memory_space=pl.ANY)
    held = pltpu.VMEM((strips, ROWS, STRIP, C), bf16)
    halo = pltpu.VMEM((strips, REACH, STRIP, C), bf16)
    wide = pltpu.VMEM((GROUPS, ROWS, cols + 2 * STRIP, CG), f32)
    ends = pltpu.VMEM((LAYERS, 2, ROWS, STRIP, C), bf16)
    dma = pltpu.SemaphoreType.DMA
    cells = 2 * fields.shape[1] * cols
    return pl.pallas_call(
        functools.partial(kernel, count, strips),
        in_specs=[hbm] * 10,
        out_specs=vmem,
        out_shape=pltpu.VMEM(fields.shape, bf16),
        scratch_shapes=[
            held,
            halo,
            halo,
            halo,
            halo,
            pltpu.VMEM((strips, ROWS + 2 * REACH, STRIP, C), bf16),
            wide,
            wide,
            ends,
            ends,
            pltpu.VMEM((2, LAYERS, TAPS, GROUPS, CG, CG), bf16),
            pltpu.VMEM((2, LAYERS, TAPS * C, C), bf16),
            pltpu.VMEM((C, HIDDEN), bf16),
            pltpu.VMEM((HIDDEN, C), bf16),
            pltpu.VMEM((BLOCKS, REACH, cols), jnp.int32),
            pltpu.VMEM((128, width), f32),
            pltpu.VMEM((width, 128), f32),
            pltpu.SMEM((LAYERS,), jnp.int32),
            pltpu.SMEM((LAYERS,), jnp.int32),
            pltpu.VMEM((LAYERS, C), f32),
            pltpu.VMEM((1, C), f32),
            dma((8, strips)),
            dma((8, strips)),
            dma((len(GROUPED), 2)),
            dma((len(GROUPED), 2)),
            dma((2,)),
            dma((2,)),
            dma((10,)),
            dma((2, strips)),
            dma((2, strips)),
        ],
        compiler_params=pltpu.CompilerParams(
            collective_id=0, has_side_effects=True, vmem_limit_bytes=VMEM_LIMIT
        ),
        cost_estimate=pl.CostEstimate(
            flops=2 * cells * (2 * LAYERS * TAPS * C * C + 2 * C * HIDDEN),
            bytes_accessed=4 * cells * C,
            transcendentals=cells * HIDDEN,
        ),
    )(
        lat_dilation,
        lon_dilation,
        fields,
        ocean,
        mix_gain,
        mlp_gain.reshape(1, C),
        lat_weight,
        lon_weight,
        w_in,
        w_out,
    )


def solution(mesh):
    return jax.shard_map(
        on_device,
        mesh=mesh,
        in_specs=(
            P("grp", "lat", "lon", None),
            P(),
            P(),
            P(),
            P(),
            P(),
            P(),
            P(),
            P(),
            P(("grp", "lat"), "lon"),
        ),
        out_specs=P("grp", "lat", "lon", None),
        check_vma=False,
    )
```

```python
import functools

import jax
import jax.numpy as jnp
from jax import lax
from jax.experimental import pallas as pl
from jax.experimental.pallas import tpu as pltpu
from jax.sharding import PartitionSpec as P

C = 256
GROUPS = 2
CG = 128
TAPS = 5
HALF = 2
LAYERS = 2
HIDDEN = 1024
REACH = 8
STRIP = 48
BLOCKS = 4
GROUPED = ((0, 0, 3), (0, 3, 1), (1, 0, 1), (1, 1, 1), (1, 2, 2))
ROWS = BLOCKS * REACH
VMEM_LIMIT = 60 * 1024 * 1024
MESH = pl.DeviceIdType.MESH
bf16 = jnp.bfloat16
f32 = jnp.float32

EDGE, REST, NEAR, FAR, NEAR2, FAR2, BACK0, BACK1 = range(8)


def scaled(wide, gain):
    power = jnp.mean(wide * wide, axis=-1, keepdims=True)
    return wide * lax.rsqrt(power + 1e-06) * gain


def kernel(
    count,
    strips,
    lat_dilation_in,
    lon_dilation_in,
    fields,
    ocean,
    mix_gain_in,
    mlp_gain_in,
    lat_weight,
    lon_weight,
    w_in,
    w_out,
    out,
    state,
    near,
    far,
    near2,
    far2,
    normed,
    wide1,
    wide2,
    halo_out,
    halo_in,
    raw,
    bank,
    v_in,
    v_out,
    sea,
    pad,
    wet,
    lat_dilation,
    lon_dilation,
    mix_gain,
    mlp_gain,
    send,
    recv,
    halo_send,
    halo_recv,
    sea_send,
    sea_recv,
    load_sem,
    own_sem,
    keep_sem,
):
    lat = lax.axis_index("lat")
    core = lax.axis_index("lon")
    member = lax.rem(lat, 2)
    other = 1 - member
    partner = {"lat": lat + 1 - 2 * member}
    across_core = {"lon": 1 - core}
    near_to = lat - 2 + 4 * member
    far_to = lat + 2 - 4 * member
    has_near_to = jnp.logical_and(near_to >= 0, near_to < count)
    has_far_to = jnp.logical_and(far_to >= 0, far_to < count)
    near_to = {"lat": near_to}
    far_to = {"lat": far_to}
    wide = (wide1, wide2)

    place = (16 - 8 * member, 24 - 24 * member, 8 + 8 * member, 24 * member)
    near_row = 40 * other
    far_row = 40 * member

    def first_col(k):
        return pl.multiple_of(STRIP * (k + core * (strips - 1 - 2 * k)), STRIP)

    def wide_col(k):
        return pl.multiple_of(STRIP * (1 + k + core * (strips - 1 - 2 * k)), STRIP)

    def halo_col(side):
        turned = side + core * (1 - 2 * side)
        return pl.multiple_of(STRIP * (strips + 1) * turned, STRIP)

    def block(b):
        return pl.ds(b * REACH, REACH)

    def part_of(ref, sample, row, k):
        return ref.at[sample, pl.ds(row, REACH), pl.ds(first_col(k), STRIP)]

    def remote(family, k, src, dst, device):
        return pltpu.make_async_remote_copy(
            src_ref=src,
            dst_ref=dst,
            send_sem=send.at[family, k],
            recv_sem=recv.at[family, k],
            device_id=device,
            device_id_type=MESH,
        )

    def edge_copy(k):
        return remote(
            EDGE, k, part_of(fields, other, REACH * member, k), state.at[k, block(1)], partner
        )

    def rest_copy(k):
        return remote(
            REST, k, part_of(fields, other, REACH * other, k), state.at[k, block(0)], partner
        )

    def near_copy(k):
        return remote(NEAR, k, part_of(fields, member, REACH * member, k), near.at[k], near_to)

    def far_copy(k):
        return remote(FAR, k, state.at[k, block(1)], far.at[k], far_to)

    def near2_copy(k):
        rows = pl.ds(REACH + place[3], REACH)
        return remote(NEAR2, k, normed.at[k, rows], near2.at[k], near_to)

    def far2_copy(k):
        rows = pl.ds(REACH + place[1], REACH)
        return remote(FAR2, k, normed.at[k, rows], far2.at[k], far_to)

    def back_copy(b, k):
        row = REACH * (member if b == 0 else other)
        return remote(
            BACK0 + b, k, state.at[k, block(b)], part_of(out, member, row, k), partner
        )

    def halo_copy(group, side):
        layer, first, number = GROUPED[group]
        rows = pl.ds(first * REACH, number * REACH)
        return pltpu.make_async_remote_copy(
            src_ref=halo_out.at[layer, side, rows],
            dst_ref=halo_in.at[layer, side, rows],
            send_sem=halo_send.at[group, side],
            recv_sem=halo_recv.at[group, side],
            device_id=across_core,
            device_id_type=MESH,
        )

    def sea_copy(b):
        row = REACH * (member if b == 1 else other)
        return pltpu.make_async_remote_copy(
            src_ref=ocean.at[pl.ds(row, REACH)],
            dst_ref=sea.at[b],
            send_sem=sea_send.at[b],
            recv_sem=sea_recv.at[b],
            device_id=partner,
            device_id_type=MESH,
        )

    def own_copy(b, k):
        row = REACH * (other if b == 2 else member)
        return pltpu.make_async_copy(
            part_of(fields, member, row, k), state.at[k, block(b)], own_sem.at[b - 2, k]
        )

    def keep_copy(b, k):
        row = REACH * (other if b == 2 else member)
        return pltpu.make_async_copy(
            state.at[k, block(b)], part_of(out, member, row, k), keep_sem.at[b - 2, k]
        )

    def sea_own(b):
        row = REACH * (other if b == 2 else member)
        return pltpu.make_async_copy(ocean.at[pl.ds(row, REACH)], sea.at[b], load_sem.at[b + 2])

    loads = (
        pltpu.make_async_copy(lat_weight, raw.at[0], load_sem.at[0]),
        pltpu.make_async_copy(lon_weight, raw.at[1], load_sem.at[1]),
        pltpu.make_async_copy(w_in, v_in, load_sem.at[2]),
        pltpu.make_async_copy(w_out, v_out, load_sem.at[3]),
        sea_own(2),
        sea_own(3),
        pltpu.make_async_copy(lat_dilation_in, lat_dilation, load_sem.at[6]),
        pltpu.make_async_copy(lon_dilation_in, lon_dilation, load_sem.at[7]),
        pltpu.make_async_copy(mix_gain_in, mix_gain, load_sem.at[8]),
        pltpu.make_async_copy(mlp_gain_in, mlp_gain, load_sem.at[9]),
    )

    barrier = pltpu.get_barrier_semaphore()
    for device, there in (
        (partner, None),
        (across_core, None),
        (near_to, has_near_to),
        (far_to, has_far_to),
    ):
        if there is None:
            pl.semaphore_signal(barrier, inc=1, device_id=device, device_id_type=MESH)
        else:

            @pl.when(there)
            def _():
                pl.semaphore_signal(barrier, inc=1, device_id=device, device_id_type=MESH)

    for copy in loads:
        copy.start()
    pl.semaphore_wait(
        barrier, 2 + has_near_to.astype(jnp.int32) + has_far_to.astype(jnp.int32)
    )

    for b in (0, 1):
        sea_copy(b).start()
    order = [edge_copy(0)]
    for k in range(strips):
        if k + 2 < strips:
            order.append(edge_copy(k + 1))
        if k + 1 == strips:
            order.append(edge_copy(k))
        order.append(rest_copy(k))
    for copy in order:
        copy.start()
    @pl.when(has_near_to)
    def _():
        for k in range(strips):
            near_copy(k).start()

    for k in range(strips):
        own_copy(2, k).start()
        own_copy(3, k).start()

    bank[...] = jnp.zeros_like(bank)
    loads[0].wait()
    loads[1].wait()
    for which in range(2):
        for layer in range(LAYERS):
            for tap in range(TAPS):
                for g in range(GROUPS):
                    at = tap * C + g * CG
                    bank[which, layer, at : at + CG, g * CG : (g + 1) * CG] = raw[
                        which, layer, tap, g
                    ]
    for copy in loads[2:]:
        copy.wait()
    pad[...] = jnp.zeros_like(pad)
    for b in range(BLOCKS):
        if b < 2:
            sea_copy(b).wait_recv()
        pad[b * REACH : (b + 1) * REACH, 0 : strips * STRIP] = sea[b].astype(f32)
    wet[...] = pad[...].T

    def put(k, row, value, gain):
        normed[k, pl.ds(row, REACH)] = scaled(value.astype(f32), gain).astype(bf16)

    def lat_conv(ks, group):
        layer, first, number = GROUPED[group]
        blocks = range(first, first + number)
        number *= REACH
        first *= REACH
        dilation = lat_dilation[layer]
        taps = []
        for tap in range(TAPS):
            pieces = []
            for k in ks:
                for b in blocks:
                    start = REACH + place[b] + (tap - HALF) * dilation
                    pieces.append(normed[k, pl.ds(start, REACH)].reshape(REACH * STRIP, C))
            taps.append(jnp.concatenate(pieces, 0))
        total = jnp.dot(
            jnp.concatenate(taps, 1), bank[0, layer], preferred_element_type=f32
        )
        total = total.astype(bf16).reshape(len(ks) * number, STRIP, C)
        for at, k in enumerate(ks):
            part = total[at * number : (at + 1) * number]
            spread(layer, first, part, wide_col(k))
            for side, end in ((0, 0), (1, strips - 1)):
                if isinstance(k, int) and k != end:
                    continue

                @pl.when(k == end)
                def _():
                    halo_out[layer, side, first : first + number] = part
                    halo_copy(group, side).start()

    def spread(layer, first, value, col):
        for g in range(GROUPS):
            wide[layer][g, pl.ds(first, value.shape[0]), pl.ds(col, STRIP), :] = value[
                :, :, g * CG : (g + 1) * CG
            ].astype(f32)

    def halo_wait(group, side):
        layer, first, number = GROUPED[group]
        halo_copy(group, side).wait_recv()
        rows = slice(first * REACH, (first + number) * REACH)
        spread(layer, first * REACH, halo_in[layer, side, rows], halo_col(side))

    def halo_check(group, k):
        for side, at in ((0, 0), (1, strips - 1)):

            @pl.when(k == at)
            def _():
                halo_wait(group, side)

    def lon_conv(layer, ks, first, number):
        dilation = lon_dilation[layer]
        taps = []
        for tap in range(TAPS):
            for g in range(GROUPS):
                pieces = []
                for k in ks:
                    start = wide_col(k) + (tap - HALF) * dilation
                    piece = wide[layer][g, pl.ds(first, number), pl.ds(start, STRIP), :]
                    pieces.append(piece.astype(bf16).reshape(number * STRIP, CG))
                taps.append(jnp.concatenate(pieces, 0))
        total = jnp.dot(
            jnp.concatenate(taps, 1), bank[1, layer], preferred_element_type=f32
        )
        values = []
        for at, k in enumerate(ks):
            mask = wet[pl.ds(first_col(k), STRIP), :]
            for r in range(number):
                old = state[k, first + r].astype(f32)
                row = (at * number + r) * STRIP
                part = total[row : row + STRIP] * mask[:, first + r : first + r + 1]
                values.append((old + part).astype(bf16))
        return values

    def early(k):
        edge_copy(k).wait_recv()

        @pl.when(has_far_to)
        def _():
            far_copy(k).start()

        own_copy(2, k).wait()
        own_copy(3, k).wait()
        for b in (1, 2, 3):
            put(k, REACH + place[b], state[k, block(b)], mix_gain[0:1])
        raw_rows(near_copy, has_far_to, near, near_row, k)

    def raw_rows(copy, there, ref, row, k):
        @pl.when(there)
        def _():
            copy(k).wait_recv()
            put(k, row, ref[k], mix_gain[0:1])

        @pl.when(jnp.logical_not(there))
        def _():
            normed[k, pl.ds(row, REACH)] = jnp.zeros((REACH, STRIP, C), bf16)

    def outer_lat(k):
        raw_rows(far_copy, has_near_to, far, far_row, k)
        lat_conv((k,), 1)

    def lon_first(k, first, number):
        values = lon_conv(0, (k,), first * REACH, number * REACH)
        for at in range(number):
            b = first + at
            part = jnp.stack(values[at * REACH : (at + 1) * REACH], 0)
            state[k, block(b)] = part
            put(k, REACH + place[b], part, mix_gain[1:2])

    def outer_lon(k):
        halo_check(1, k)
        lon_first(k, 3, 1)

        @pl.when(has_near_to)
        def _():
            near2_copy(k).start()

    def finish(ks, first, number):
        new = jnp.concatenate(lon_conv(1, ks, first, number), 0).astype(f32)
        lifted = scaled(new, mlp_gain[...]).astype(bf16)
        half = 0.5 * jnp.dot(lifted, v_in[...], preferred_element_type=f32)
        hidden = (half + half * jnp.tanh(half)).astype(bf16)
        update = jnp.dot(hidden, v_out[...], preferred_element_type=f32)
        result = (new + update).astype(bf16).reshape(len(ks) * number, STRIP, C)
        for at, k in enumerate(ks):
            state[k, first : first + number] = result[at * number : (at + 1) * number]

    early(0)

    def step(k, carry):
        @pl.when(k + 2 < strips)
        def _():
            early(k + 1)

        @pl.when(k + 1 == strips)
        def _():
            early(k)

        before = k - (k + 1) // strips

        @pl.when(jnp.logical_or(k + 2 < strips, k + 1 == strips))
        def _():
            outer_lat(before)

        @pl.when(jnp.logical_and(k >= 1, jnp.logical_or(k + 2 < strips, k + 1 == strips)))
        def _():
            outer_lon(before - 1)

        @pl.when(k < strips)
        def _():
            rest_copy(k).wait_recv()
            put(k, REACH + place[0], state[k, block(0)], mix_gain[0:1])
            lat_conv((k,), 0)

        @pl.when(jnp.logical_and(k >= 1, k <= strips))
        def _():
            j = k - 1
            halo_check(0, j)

            @pl.when(has_far_to)
            def _():
                far_copy(j).wait_send()

            lon_first(j, 0, 3)

            @pl.when(has_far_to)
            def _():
                far2_copy(j).start()

            lat_conv((j,), 2)

        @pl.when(k >= 2)
        def _():
            i = k - 2
            halo_check(2, i)
            finish((i,), 0, REACH)
            back_copy(0, i).start()

        @pl.when(k == strips - 1)
        def _():
            outer_lat(k)

        @pl.when(k >= strips)
        def _():
            outer_lon(k - 2)

        return carry

    lax.fori_loop(0, strips + 2, step, 0)

    def halo_rows(copy, there, ref, row, k):
        @pl.when(there)
        def _():
            copy(k).wait_recv()
            normed[k, pl.ds(row, REACH)] = ref[k]

        @pl.when(jnp.logical_not(there))
        def _():
            normed[k, pl.ds(row, REACH)] = jnp.zeros((REACH, STRIP, C), bf16)

    def edge_step(k, carry):
        @pl.when(k < strips)
        def _():
            halo_rows(near2_copy, has_far_to, near2, near_row, k)
            lat_conv((k,), 3)

        @pl.when(k >= 1)
        def _():
            halo_check(3, k - 1)
            finish((k - 1,), REACH, REACH)
            back_copy(1, k - 1).start()

        @pl.when(k < strips)
        def _():
            halo_rows(far2_copy, has_near_to, far2, far_row, k)
            lat_conv((k,), 4)

        return carry

    def keep_step(k, carry):
        halo_check(4, k)
        finish((k,), 2 * REACH, 2 * REACH)
        keep_copy(2, k).start()
        keep_copy(3, k).start()
        return carry

    lax.fori_loop(0, strips + 1, edge_step, 0)
    lax.fori_loop(0, strips, keep_step, 0)

    for group in range(len(GROUPED)):
        for side in range(2):
            halo_copy(group, side).wait_send()
    for b in (0, 1):
        sea_copy(b).wait_send()
    for k in range(strips):
        edge_copy(k).wait_send()
        rest_copy(k).wait_send()

        @pl.when(has_near_to)
        def _():
            near_copy(k).wait_send()
            near2_copy(k).wait_send()

        @pl.when(has_far_to)
        def _():
            far2_copy(k).wait_send()

        keep_copy(2, k).wait()
        keep_copy(3, k).wait()
        back_copy(0, k).wait()
        back_copy(1, k).wait()


def on_device(
    fields,
    mix_gain,
    lat_weight,
    lon_weight,
    mlp_gain,
    w_in,
    w_out,
    lat_dilation,
    lon_dilation,
    ocean,
):
    cols = fields.shape[2]
    strips = cols // STRIP
    count = lax.axis_size("lat")
    width = -(-cols // 128) * 128
    vmem = pl.BlockSpec(memory_space=pltpu.VMEM)
    hbm = pl.BlockSpec(memory_space=pl.ANY)
    held = pltpu.VMEM((strips, ROWS, STRIP, C), bf16)
    halo = pltpu.VMEM((strips, REACH, STRIP, C), bf16)
    wide = pltpu.VMEM((GROUPS, ROWS, cols + 2 * STRIP, CG), f32)
    ends = pltpu.VMEM((LAYERS, 2, ROWS, STRIP, C), bf16)
    dma = pltpu.SemaphoreType.DMA
    cells = 2 * fields.shape[1] * cols
    return pl.pallas_call(
        functools.partial(kernel, count, strips),
        in_specs=[hbm] * 10,
        out_specs=vmem,
        out_shape=pltpu.VMEM(fields.shape, bf16),
        scratch_shapes=[
            held,
            halo,
            halo,
            halo,
            halo,
            pltpu.VMEM((strips, ROWS + 2 * REACH, STRIP, C), bf16),
            wide,
            wide,
            ends,
            ends,
            pltpu.VMEM((2, LAYERS, TAPS, GROUPS, CG, CG), bf16),
            pltpu.VMEM((2, LAYERS, TAPS * C, C), bf16),
            pltpu.VMEM((C, HIDDEN), bf16),
            pltpu.VMEM((HIDDEN, C), bf16),
            pltpu.VMEM((BLOCKS, REACH, cols), jnp.int32),
            pltpu.VMEM((128, width), f32),
            pltpu.VMEM((width, 128), f32),
            pltpu.SMEM((LAYERS,), jnp.int32),
            pltpu.SMEM((LAYERS,), jnp.int32),
            pltpu.VMEM((LAYERS, C), f32),
            pltpu.VMEM((1, C), f32),
            dma((8, strips)),
            dma((8, strips)),
            dma((len(GROUPED), 2)),
            dma((len(GROUPED), 2)),
            dma((2,)),
            dma((2,)),
            dma((10,)),
            dma((2, strips)),
            dma((2, strips)),
        ],
        compiler_params=pltpu.CompilerParams(
            collective_id=0, has_side_effects=True, vmem_limit_bytes=VMEM_LIMIT
        ),
        cost_estimate=pl.CostEstimate(
            flops=2 * cells * (2 * LAYERS * TAPS * C * C + 2 * C * HIDDEN),
            bytes_accessed=4 * cells * C,
            transcendentals=cells * HIDDEN,
        ),
    )(
        lat_dilation,
        lon_dilation,
        fields,
        ocean,
        mix_gain,
        mlp_gain.reshape(1, C),
        lat_weight,
        lon_weight,
        w_in,
        w_out,
    )


def solution(mesh):
    return jax.shard_map(
        on_device,
        mesh=mesh,
        in_specs=(
            P("grp", "lat", "lon", None),
            P(),
            P(),
            P(),
            P(),
            P(),
            P(),
            P(),
            P(),
            P(("grp", "lat"), "lon"),
        ),
        out_specs=P("grp", "lat", "lon", None),
        check_vma=False,
    )
```

```python
import functools

import jax
import jax.numpy as jnp
from jax import lax
from jax.experimental import pallas as pl
from jax.experimental.pallas import tpu as pltpu
from jax.sharding import PartitionSpec as P

C = 256
GROUPS = 2
CG = 128
TAPS = 5
HALF = 2
LAYERS = 2
HIDDEN = 1024
REACH = 8
STRIP = 48
BLOCKS = 4
GROUPED = ((0, 0, 3), (0, 3, 1), (1, 0, 1), (1, 1, 1), (1, 2, 2))
ROWS = BLOCKS * REACH
VMEM_LIMIT = 60 * 1024 * 1024
MESH = pl.DeviceIdType.MESH
bf16 = jnp.bfloat16
f32 = jnp.float32

EDGE, REST, NEAR, FAR, NEAR2, FAR2, BACK0, BACK1 = range(8)


def scaled(wide, gain):
    power = jnp.mean(wide * wide, axis=-1, keepdims=True)
    return wide * lax.rsqrt(power + 1e-06) * gain


def kernel(
    count,
    strips,
    lat_dilation_in,
    lon_dilation_in,
    fields,
    ocean,
    mix_gain_in,
    mlp_gain_in,
    lat_weight,
    lon_weight,
    w_in,
    w_out,
    out,
    state,
    near,
    far,
    near2,
    far2,
    normed,
    wide1,
    wide2,
    halo_out,
    halo_in,
    raw,
    bank,
    v_in,
    v_out,
    sea,
    pad,
    wet,
    lat_dilation,
    lon_dilation,
    mix_gain,
    mlp_gain,
    send,
    recv,
    halo_send,
    halo_recv,
    sea_send,
    sea_recv,
    load_sem,
    own_sem,
    keep_sem,
):
    lat = lax.axis_index("lat")
    core = lax.axis_index("lon")
    member = lax.rem(lat, 2)
    other = 1 - member
    partner = {"lat": lat + 1 - 2 * member}
    across_core = {"lon": 1 - core}
    near_to = lat - 2 + 4 * member
    far_to = lat + 2 - 4 * member
    has_near_to = jnp.logical_and(near_to >= 0, near_to < count)
    has_far_to = jnp.logical_and(far_to >= 0, far_to < count)
    near_to = {"lat": near_to}
    far_to = {"lat": far_to}
    wide = (wide1, wide2)

    place = (16 - 8 * member, 24 - 24 * member, 8 + 8 * member, 24 * member)

    def where(b):
        if isinstance(b, int):
            return place[b]
        return 16 - 8 * member + b * (8 - 16 * member)

    near_row = 40 * other
    far_row = 40 * member

    def first_col(k):
        return pl.multiple_of(STRIP * (k + core * (strips - 1 - 2 * k)), STRIP)

    def wide_col(k):
        return pl.multiple_of(STRIP * (1 + k + core * (strips - 1 - 2 * k)), STRIP)

    def halo_col(side):
        turned = side + core * (1 - 2 * side)
        return pl.multiple_of(STRIP * (strips + 1) * turned, STRIP)

    def block(b):
        return pl.ds(b * REACH, REACH)

    def part_of(ref, sample, row, k):
        return ref.at[sample, pl.ds(row, REACH), pl.ds(first_col(k), STRIP)]

    def remote(family, k, src, dst, device):
        return pltpu.make_async_remote_copy(
            src_ref=src,
            dst_ref=dst,
            send_sem=send.at[family, k],
            recv_sem=recv.at[family, k],
            device_id=device,
            device_id_type=MESH,
        )

    def edge_copy(k):
        return remote(
            EDGE, k, part_of(fields, other, REACH * member, k), state.at[k, block(1)], partner
        )

    def rest_copy(k):
        return remote(
            REST, k, part_of(fields, other, REACH * other, k), state.at[k, block(0)], partner
        )

    def near_copy(k):
        return remote(NEAR, k, part_of(fields, member, REACH * member, k), near.at[k], near_to)

    def far_copy(k):
        return remote(FAR, k, state.at[k, block(1)], far.at[k], far_to)

    def near2_copy(k):
        rows = pl.ds(REACH + place[3], REACH)
        return remote(NEAR2, k, normed.at[k, rows], near2.at[k], near_to)

    def far2_copy(k):
        rows = pl.ds(REACH + place[1], REACH)
        return remote(FAR2, k, normed.at[k, rows], far2.at[k], far_to)

    def back_copy(b, k):
        row = REACH * (member + b * (1 - 2 * member))
        return remote(
            BACK0 + b, k, state.at[k, block(b)], part_of(out, member, row, k), partner
        )

    def group_of(group):
        if isinstance(group, int):
            return GROUPED[group]
        return 1, group - 2, 1

    def halo_copy(group, side):
        layer, first, number = group_of(group)
        rows = pl.ds(first * REACH, number * REACH)
        return pltpu.make_async_remote_copy(
            src_ref=halo_out.at[layer, side, rows],
            dst_ref=halo_in.at[layer, side, rows],
            send_sem=halo_send.at[group, side],
            recv_sem=halo_recv.at[group, side],
            device_id=across_core,
            device_id_type=MESH,
        )

    def sea_copy(b):
        row = REACH * (member if b == 1 else other)
        return pltpu.make_async_remote_copy(
            src_ref=ocean.at[pl.ds(row, REACH)],
            dst_ref=sea.at[b],
            send_sem=sea_send.at[b],
            recv_sem=sea_recv.at[b],
            device_id=partner,
            device_id_type=MESH,
        )

    def own_copy(b, k):
        row = REACH * (other if b == 2 else member)
        return pltpu.make_async_copy(
            part_of(fields, member, row, k), state.at[k, block(b)], own_sem.at[b - 2, k]
        )

    def keep_copy(b, k):
        row = REACH * (other if b == 2 else member)
        return pltpu.make_async_copy(
            state.at[k, block(b)], part_of(out, member, row, k), keep_sem.at[b - 2, k]
        )

    def sea_own(b):
        row = REACH * (other if b == 2 else member)
        return pltpu.make_async_copy(ocean.at[pl.ds(row, REACH)], sea.at[b], load_sem.at[b + 2])

    loads = (
        pltpu.make_async_copy(lat_weight, raw.at[0], load_sem.at[0]),
        pltpu.make_async_copy(lon_weight, raw.at[1], load_sem.at[1]),
        pltpu.make_async_copy(w_in, v_in, load_sem.at[2]),
        pltpu.make_async_copy(w_out, v_out, load_sem.at[3]),
        sea_own(2),
        sea_own(3),
        pltpu.make_async_copy(lat_dilation_in, lat_dilation, load_sem.at[6]),
        pltpu.make_async_copy(lon_dilation_in, lon_dilation, load_sem.at[7]),
        pltpu.make_async_copy(mix_gain_in, mix_gain, load_sem.at[8]),
        pltpu.make_async_copy(mlp_gain_in, mlp_gain, load_sem.at[9]),
    )

    barrier = pltpu.get_barrier_semaphore()
    for device, there in (
        (partner, None),
        (across_core, None),
        (near_to, has_near_to),
        (far_to, has_far_to),
    ):
        if there is None:
            pl.semaphore_signal(barrier, inc=1, device_id=device, device_id_type=MESH)
        else:

            @pl.when(there)
            def _():
                pl.semaphore_signal(barrier, inc=1, device_id=device, device_id_type=MESH)

    for copy in loads:
        copy.start()
    pl.semaphore_wait(
        barrier, 2 + has_near_to.astype(jnp.int32) + has_far_to.astype(jnp.int32)
    )

    for b in (0, 1):
        sea_copy(b).start()
    order = [edge_copy(0)]
    for k in range(strips):
        if k + 2 < strips:
            order.append(edge_copy(k + 1))
        if k + 1 == strips:
            order.append(edge_copy(k))
        order.append(rest_copy(k))
    for copy in order:
        copy.start()
    @pl.when(has_near_to)
    def _():
        for k in range(strips):
            near_copy(k).start()

    for k in range(strips):
        own_copy(2, k).start()
        own_copy(3, k).start()

    bank[...] = jnp.zeros_like(bank)
    loads[0].wait()
    loads[1].wait()
    for which in range(2):
        for layer in range(LAYERS):
            for tap in range(TAPS):
                for g in range(GROUPS):
                    at = tap * C + g * CG
                    bank[which, layer, at : at + CG, g * CG : (g + 1) * CG] = raw[
                        which, layer, tap, g
                    ]
    for copy in loads[2:]:
        copy.wait()
    pad[...] = jnp.zeros_like(pad)
    for b in range(BLOCKS):
        if b < 2:
            sea_copy(b).wait_recv()
        pad[0:REACH, 0 : strips * STRIP] = sea[b].astype(f32)
        wet[b] = pad[...].T

    def put(k, row, value, gain):
        normed[k, pl.ds(row, REACH)] = scaled(value.astype(f32), gain).astype(bf16)

    def lat_conv(ks, group):
        layer, first, number = group_of(group)
        rows = [where(first + at) for at in range(number)]
        number *= REACH
        first = first * REACH
        dilation = lat_dilation[layer]
        taps = []
        for tap in range(TAPS):
            pieces = []
            for k in ks:
                for row in rows:
                    start = REACH + row + (tap - HALF) * dilation
                    pieces.append(normed[k, pl.ds(start, REACH)].reshape(REACH * STRIP, C))
            taps.append(jnp.concatenate(pieces, 0))
        total = jnp.dot(
            jnp.concatenate(taps, 1), bank[0, layer], preferred_element_type=f32
        )
        total = total.astype(bf16).reshape(len(ks) * number, STRIP, C)
        for at, k in enumerate(ks):
            part = total[at * number : (at + 1) * number]
            spread(layer, first, part, wide_col(k))
            for side, end in ((0, 0), (1, strips - 1)):
                if isinstance(k, int) and k != end:
                    continue

                @pl.when(k == end)
                def _():
                    halo_out[layer, side, pl.ds(first, number)] = part
                    halo_copy(group, side).start()

    def spread(layer, first, value, col):
        for g in range(GROUPS):
            wide[layer][g, pl.ds(first, value.shape[0]), pl.ds(col, STRIP), :] = value[
                :, :, g * CG : (g + 1) * CG
            ].astype(f32)

    def halo_wait(group, side):
        layer, first, number = group_of(group)
        halo_copy(group, side).wait_recv()
        rows = pl.ds(first * REACH, number * REACH)
        spread(layer, first * REACH, halo_in[layer, side, rows], halo_col(side))

    def halo_check(group, k):
        for side, at in ((0, 0), (1, strips - 1)):

            @pl.when(k == at)
            def _():
                halo_wait(group, side)

    def lon_conv(layer, ks, first_block, number):
        first = first_block * REACH
        dilation = lon_dilation[layer]
        taps = []
        for tap in range(TAPS):
            for g in range(GROUPS):
                pieces = []
                for k in ks:
                    start = wide_col(k) + (tap - HALF) * dilation
                    piece = wide[layer][g, pl.ds(first, number), pl.ds(start, STRIP), :]
                    pieces.append(piece.astype(bf16).reshape(number * STRIP, CG))
                taps.append(jnp.concatenate(pieces, 0))
        total = jnp.dot(
            jnp.concatenate(taps, 1), bank[1, layer], preferred_element_type=f32
        )
        values = []
        for at, k in enumerate(ks):
            for part in range(number // REACH):
                mask = wet[first_block + part, pl.ds(first_col(k), STRIP), :]
                for r in range(REACH):
                    line = part * REACH + r
                    old = state[k, first + line].astype(f32)
                    row = (at * number + line) * STRIP
                    piece = total[row : row + STRIP] * mask[:, r : r + 1]
                    values.append((old + piece).astype(bf16))
        return values

    def early(k):
        edge_copy(k).wait_recv()

        @pl.when(has_far_to)
        def _():
            far_copy(k).start()

        own_copy(2, k).wait()
        own_copy(3, k).wait()
        for b in (1, 2, 3):
            put(k, REACH + place[b], state[k, block(b)], mix_gain[0:1])
        raw_rows(near_copy, has_far_to, near, near_row, k)

    def raw_rows(copy, there, ref, row, k):
        @pl.when(there)
        def _():
            copy(k).wait_recv()
            put(k, row, ref[k], mix_gain[0:1])

        @pl.when(jnp.logical_not(there))
        def _():
            normed[k, pl.ds(row, REACH)] = jnp.zeros((REACH, STRIP, C), bf16)

    def outer_lat(k):
        raw_rows(far_copy, has_near_to, far, far_row, k)
        lat_conv((k,), 1)

    def lon_first(k, first, number):
        values = lon_conv(0, (k,), first, number * REACH)
        for at in range(number):
            b = first + at
            part = jnp.stack(values[at * REACH : (at + 1) * REACH], 0)
            state[k, block(b)] = part
            put(k, REACH + place[b], part, mix_gain[1:2])

    def outer_lon(k):
        halo_check(1, k)
        lon_first(k, 3, 1)

        @pl.when(has_near_to)
        def _():
            near2_copy(k).start()

    def finish(ks, first_block, number):
        first = first_block * REACH
        new = jnp.concatenate(lon_conv(1, ks, first_block, number), 0).astype(f32)
        lifted = scaled(new, mlp_gain[...]).astype(bf16)
        half = 0.5 * jnp.dot(lifted, v_in[...], preferred_element_type=f32)
        hidden = (half + half * jnp.tanh(half)).astype(bf16)
        update = jnp.dot(hidden, v_out[...], preferred_element_type=f32)
        result = (new + update).astype(bf16).reshape(len(ks) * number, STRIP, C)
        for at, k in enumerate(ks):
            state[k, pl.ds(first, number)] = result[at * number : (at + 1) * number]

    def halo_rows(copy, there, ref, row, k):
        @pl.when(there)
        def _():
            copy(k).wait_recv()
            normed[k, pl.ds(row, REACH)] = ref[k]

        @pl.when(jnp.logical_not(there))
        def _():
            normed[k, pl.ds(row, REACH)] = jnp.zeros((REACH, STRIP, C), bf16)

    early(0)

    def step(k, carry):
        @pl.when(k + 2 < strips)
        def _():
            early(k + 1)

        @pl.when(k + 1 == strips)
        def _():
            early(k)

        before = jnp.where(k + 1 == strips, k - 1, k)

        @pl.when(jnp.logical_or(k + 2 < strips, k + 1 == strips))
        def _():
            outer_lat(before)

        @pl.when(jnp.logical_and(k >= 1, jnp.logical_or(k + 2 < strips, k + 1 == strips)))
        def _():
            outer_lon(before - 1)

        @pl.when(k < strips)
        def _():
            rest_copy(k).wait_recv()
            put(k, REACH + place[0], state[k, block(0)], mix_gain[0:1])
            lat_conv((k,), 0)

        @pl.when(jnp.logical_and(k >= 1, k <= strips))
        def _():
            j = k - 1
            halo_check(0, j)

            @pl.when(has_far_to)
            def _():
                far_copy(j).wait_send()

            lon_first(j, 0, 3)

            @pl.when(has_far_to)
            def _():
                far2_copy(j).start()

        edge = (k >= strips + 2).astype(jnp.int32)
        at = k - edge * (strips + 2)

        @pl.when(jnp.logical_and(edge == 1, at < strips))
        def _():
            halo_rows(near2_copy, has_far_to, near2, near_row, at)

        j = k - 1 - edge * (strips + 1)

        @pl.when(jnp.logical_and(j >= 0, j < strips))
        def _():
            lat_conv((j,), 2 + edge)

        i = k - 2 - edge * (strips + 1)

        @pl.when(jnp.logical_and(i >= 0, i < strips))
        def _():
            halo_check(2 + edge, i)
            finish((i,), edge, REACH)
            back_copy(edge, i).start()

        @pl.when(jnp.logical_and(edge == 1, at < strips))
        def _():
            halo_rows(far2_copy, has_near_to, far2, far_row, at)
            lat_conv((at,), 4)

        @pl.when(k == strips - 1)
        def _():
            outer_lat(k)

        @pl.when(jnp.logical_or(k == strips, k == strips + 1))
        def _():
            outer_lon(k - 2)

        return carry

    lax.fori_loop(0, 2 * strips + 3, step, 0)

    for side in range(2):
        halo_wait(4, side)

    def keep_step(pair, carry):
        ks = (2 * pair, 2 * pair + 1)
        finish(ks, 2, 2 * REACH)
        for k in ks:
            keep_copy(2, k).start()
            keep_copy(3, k).start()
        return carry

    lax.fori_loop(0, strips // 2, keep_step, 0)

    for group in range(len(GROUPED)):
        for side in range(2):
            halo_copy(group, side).wait_send()
    for b in (0, 1):
        sea_copy(b).wait_send()
    for k in range(strips):
        edge_copy(k).wait_send()
        rest_copy(k).wait_send()

        @pl.when(has_near_to)
        def _():
            near_copy(k).wait_send()
            near2_copy(k).wait_send()

        @pl.when(has_far_to)
        def _():
            far2_copy(k).wait_send()

        keep_copy(2, k).wait()
        keep_copy(3, k).wait()
        back_copy(0, k).wait()
        back_copy(1, k).wait()


def on_device(
    fields,
    mix_gain,
    lat_weight,
    lon_weight,
    mlp_gain,
    w_in,
    w_out,
    lat_dilation,
    lon_dilation,
    ocean,
):
    cols = fields.shape[2]
    strips = cols // STRIP
    count = lax.axis_size("lat")
    width = -(-cols // 128) * 128
    vmem = pl.BlockSpec(memory_space=pltpu.VMEM)
    hbm = pl.BlockSpec(memory_space=pl.ANY)
    held = pltpu.VMEM((strips, ROWS, STRIP, C), bf16)
    halo = pltpu.VMEM((strips, REACH, STRIP, C), bf16)
    wide = pltpu.VMEM((GROUPS, ROWS, cols + 2 * STRIP, CG), f32)
    ends = pltpu.VMEM((LAYERS, 2, ROWS, STRIP, C), bf16)
    dma = pltpu.SemaphoreType.DMA
    cells = 2 * fields.shape[1] * cols
    return pl.pallas_call(
        functools.partial(kernel, count, strips),
        in_specs=[hbm] * 10,
        out_specs=vmem,
        out_shape=pltpu.VMEM(fields.shape, bf16),
        scratch_shapes=[
            held,
            halo,
            halo,
            halo,
            halo,
            pltpu.VMEM((strips, ROWS + 2 * REACH, STRIP, C), bf16),
            wide,
            wide,
            ends,
            ends,
            pltpu.VMEM((2, LAYERS, TAPS, GROUPS, CG, CG), bf16),
            pltpu.VMEM((2, LAYERS, TAPS * C, C), bf16),
            pltpu.VMEM((C, HIDDEN), bf16),
            pltpu.VMEM((HIDDEN, C), bf16),
            pltpu.VMEM((BLOCKS, REACH, cols), jnp.int32),
            pltpu.VMEM((128, width), f32),
            pltpu.VMEM((BLOCKS, width, 128), f32),
            pltpu.SMEM((LAYERS,), jnp.int32),
            pltpu.SMEM((LAYERS,), jnp.int32),
            pltpu.VMEM((LAYERS, C), f32),
            pltpu.VMEM((1, C), f32),
            dma((8, strips)),
            dma((8, strips)),
            dma((len(GROUPED), 2)),
            dma((len(GROUPED), 2)),
            dma((2,)),
            dma((2,)),
            dma((10,)),
            dma((2, strips)),
            dma((2, strips)),
        ],
        compiler_params=pltpu.CompilerParams(
            collective_id=0, has_side_effects=True, vmem_limit_bytes=VMEM_LIMIT
        ),
        cost_estimate=pl.CostEstimate(
            flops=2 * cells * (2 * LAYERS * TAPS * C * C + 2 * C * HIDDEN),
            bytes_accessed=4 * cells * C,
            transcendentals=cells * HIDDEN,
        ),
    )(
        lat_dilation,
        lon_dilation,
        fields,
        ocean,
        mix_gain,
        mlp_gain.reshape(1, C),
        lat_weight,
        lon_weight,
        w_in,
        w_out,
    )


def solution(mesh):
    return jax.shard_map(
        on_device,
        mesh=mesh,
        in_specs=(
            P("grp", "lat", "lon", None),
            P(),
            P(),
            P(),
            P(),
            P(),
            P(),
            P(),
            P(),
            P(("grp", "lat"), "lon"),
        ),
        out_specs=P("grp", "lat", "lon", None),
        check_vma=False,
    )
```

```python
import functools

import jax
import jax.numpy as jnp
from jax import lax
from jax.experimental import pallas as pl
from jax.experimental.pallas import tpu as pltpu
from jax.sharding import PartitionSpec as P

C = 256
GROUPS = 2
CG = 128
TAPS = 5
HALF = 2
LAYERS = 2
HIDDEN = 1024
REACH = 8
STRIP = 48
BLOCKS = 4
GROUPED = ((0, 0, 3), (0, 3, 1), (1, 0, 1), (1, 1, 1), (1, 2, 2))
ROWS = BLOCKS * REACH
VMEM_LIMIT = 60 * 1024 * 1024
MESH = pl.DeviceIdType.MESH
bf16 = jnp.bfloat16
f32 = jnp.float32

EDGE, REST, NEAR, FAR, NEAR2, FAR2, BACK0, BACK1 = range(8)


def scaled(wide, gain):
    power = jnp.mean(wide * wide, axis=-1, keepdims=True)
    return wide * lax.rsqrt(power + 1e-06) * gain


def kernel(
    count,
    strips,
    lat_dilation_in,
    lon_dilation_in,
    fields,
    ocean,
    mix_gain_in,
    mlp_gain_in,
    lat_weight,
    lon_weight,
    w_in,
    w_out,
    out,
    state,
    near,
    far,
    near2,
    far2,
    normed,
    wide1,
    wide2,
    halo_out,
    halo_in,
    raw,
    bank,
    v_in,
    v_out,
    sea,
    pad,
    wet,
    lat_dilation,
    lon_dilation,
    mix_gain,
    mlp_gain,
    send,
    recv,
    halo_send,
    halo_recv,
    sea_send,
    sea_recv,
    load_sem,
    own_sem,
):
    lat = lax.axis_index("lat")
    core = lax.axis_index("lon")
    member = lax.rem(lat, 2)
    other = 1 - member
    partner = {"lat": lat + 1 - 2 * member}
    across_core = {"lon": 1 - core}
    near_to = lat - 2 + 4 * member
    far_to = lat + 2 - 4 * member
    has_near_to = jnp.logical_and(near_to >= 0, near_to < count)
    has_far_to = jnp.logical_and(far_to >= 0, far_to < count)
    near_to = {"lat": near_to}
    far_to = {"lat": far_to}
    wide = (wide1, wide2)

    place = (16 - 8 * member, 24 - 24 * member, 8 + 8 * member, 24 * member)

    def where(b):
        if isinstance(b, int):
            return place[b]
        return 16 - 8 * member + b * (8 - 16 * member)

    near_row = 40 * other
    far_row = 40 * member

    def first_col(k):
        return pl.multiple_of(STRIP * (k + core * (strips - 1 - 2 * k)), STRIP)

    def wide_col(k):
        return pl.multiple_of(STRIP * (1 + k + core * (strips - 1 - 2 * k)), STRIP)

    def halo_col(side):
        turned = side + core * (1 - 2 * side)
        return pl.multiple_of(STRIP * (strips + 1) * turned, STRIP)

    def block(b):
        return pl.ds(b * REACH, REACH)

    def part_of(ref, sample, row, k):
        return ref.at[sample, pl.ds(row, REACH), pl.ds(first_col(k), STRIP)]

    def remote(family, k, src, dst, device):
        return pltpu.make_async_remote_copy(
            src_ref=src,
            dst_ref=dst,
            send_sem=send.at[family, k],
            recv_sem=recv.at[family, k],
            device_id=device,
            device_id_type=MESH,
        )

    def edge_copy(k):
        return remote(
            EDGE, k, part_of(fields, other, REACH * member, k), state.at[k, block(1)], partner
        )

    def rest_copy(k):
        return remote(
            REST, k, part_of(fields, other, REACH * other, k), state.at[k, block(0)], partner
        )

    def near_copy(k):
        return remote(NEAR, k, part_of(fields, member, REACH * member, k), near.at[k], near_to)

    def far_copy(k):
        return remote(FAR, k, state.at[k, block(1)], far.at[k], far_to)

    def near2_copy(k):
        rows = pl.ds(REACH + place[3], REACH)
        return remote(NEAR2, k, normed.at[k, rows], near2.at[k], near_to)

    def far2_copy(k):
        rows = pl.ds(REACH + place[1], REACH)
        return remote(FAR2, k, normed.at[k, rows], far2.at[k], far_to)

    def back_copy(b, k):
        row = REACH * (member + b * (1 - 2 * member))
        return remote(
            BACK0 + b, k, state.at[k, block(b)], part_of(out, member, row, k), partner
        )

    def group_of(group):
        if isinstance(group, int):
            return GROUPED[group]
        return 1, group - 2, 1

    def halo_copy(group, side):
        layer, first, number = group_of(group)
        rows = pl.ds(first * REACH, number * REACH)
        return pltpu.make_async_remote_copy(
            src_ref=halo_out.at[layer, side, rows],
            dst_ref=halo_in.at[layer, side, rows],
            send_sem=halo_send.at[group, side],
            recv_sem=halo_recv.at[group, side],
            device_id=across_core,
            device_id_type=MESH,
        )

    def sea_copy(b):
        row = REACH * (member if b == 1 else other)
        return pltpu.make_async_remote_copy(
            src_ref=ocean.at[pl.ds(row, REACH)],
            dst_ref=sea.at[b],
            send_sem=sea_send.at[b],
            recv_sem=sea_recv.at[b],
            device_id=partner,
            device_id_type=MESH,
        )

    def own_copy(b, k):
        row = REACH * (other if b == 2 else member)
        return pltpu.make_async_copy(
            part_of(fields, member, row, k), state.at[k, block(b)], own_sem.at[b - 2, k]
        )

    def sea_own(b):
        row = REACH * (other if b == 2 else member)
        return pltpu.make_async_copy(ocean.at[pl.ds(row, REACH)], sea.at[b], load_sem.at[b + 2])

    loads = (
        pltpu.make_async_copy(lat_weight, raw.at[0], load_sem.at[0]),
        pltpu.make_async_copy(lon_weight, raw.at[1], load_sem.at[1]),
        pltpu.make_async_copy(w_in, v_in, load_sem.at[2]),
        pltpu.make_async_copy(w_out, v_out, load_sem.at[3]),
        sea_own(2),
        sea_own(3),
        pltpu.make_async_copy(lat_dilation_in, lat_dilation, load_sem.at[6]),
        pltpu.make_async_copy(lon_dilation_in, lon_dilation, load_sem.at[7]),
        pltpu.make_async_copy(mix_gain_in, mix_gain, load_sem.at[8]),
        pltpu.make_async_copy(mlp_gain_in, mlp_gain, load_sem.at[9]),
    )

    barrier = pltpu.get_barrier_semaphore()
    for device, there in (
        (partner, None),
        (across_core, None),
        (near_to, has_near_to),
        (far_to, has_far_to),
    ):
        if there is None:
            pl.semaphore_signal(barrier, inc=1, device_id=device, device_id_type=MESH)
        else:

            @pl.when(there)
            def _():
                pl.semaphore_signal(barrier, inc=1, device_id=device, device_id_type=MESH)

    for copy in loads:
        copy.start()
    pl.semaphore_wait(
        barrier, 2 + has_near_to.astype(jnp.int32) + has_far_to.astype(jnp.int32)
    )

    for b in (0, 1):
        sea_copy(b).start()
    order = [edge_copy(0)]
    for k in range(strips):
        if k + 2 < strips:
            order.append(edge_copy(k + 1))
        if k + 1 == strips:
            order.append(edge_copy(k))
        order.append(rest_copy(k))
    for copy in order:
        copy.start()
    @pl.when(has_near_to)
    def _():
        for k in range(strips):
            near_copy(k).start()

    for k in range(strips):
        own_copy(2, k).start()
        own_copy(3, k).start()

    bank[...] = jnp.zeros_like(bank)
    loads[0].wait()
    loads[1].wait()
    for which in range(2):
        for layer in range(LAYERS):
            for tap in range(TAPS):
                for g in range(GROUPS):
                    at = tap * C + g * CG
                    bank[which, layer, at : at + CG, g * CG : (g + 1) * CG] = raw[
                        which, layer, tap, g
                    ]
    for copy in loads[2:]:
        copy.wait()
    pad[...] = jnp.zeros_like(pad)
    for b in range(BLOCKS):
        if b < 2:
            sea_copy(b).wait_recv()
        pad[0:REACH, 0 : strips * STRIP] = sea[b].astype(f32)
        wet[b] = pad[...].T

    def put(k, row, value, gain):
        normed[k, pl.ds(row, REACH)] = scaled(value.astype(f32), gain).astype(bf16)

    def lat_conv(ks, group):
        layer, first, number = group_of(group)
        rows = [where(first + at) for at in range(number)]
        number *= REACH
        first = first * REACH
        dilation = lat_dilation[layer]
        taps = []
        for tap in range(TAPS):
            pieces = []
            for k in ks:
                for row in rows:
                    start = REACH + row + (tap - HALF) * dilation
                    pieces.append(normed[k, pl.ds(start, REACH)].reshape(REACH * STRIP, C))
            taps.append(jnp.concatenate(pieces, 0))
        total = jnp.dot(
            jnp.concatenate(taps, 1), bank[0, layer], preferred_element_type=f32
        )
        total = total.astype(bf16).reshape(len(ks) * number, STRIP, C)
        for at, k in enumerate(ks):
            part = total[at * number : (at + 1) * number]
            spread(layer, first, part, wide_col(k))
            for side, end in ((0, 0), (1, strips - 1)):
                if isinstance(k, int) and k != end:
                    continue

                @pl.when(k == end)
                def _():
                    halo_out[layer, side, pl.ds(first, number)] = part
                    halo_copy(group, side).start()

    def spread(layer, first, value, col):
        for g in range(GROUPS):
            wide[layer][g, pl.ds(first, value.shape[0]), pl.ds(col, STRIP), :] = value[
                :, :, g * CG : (g + 1) * CG
            ].astype(f32)

    def halo_wait(group, side):
        layer, first, number = group_of(group)
        halo_copy(group, side).wait_recv()
        rows = pl.ds(first * REACH, number * REACH)
        spread(layer, first * REACH, halo_in[layer, side, rows], halo_col(side))

    def halo_check(group, k):
        for side, at in ((0, 0), (1, strips - 1)):

            @pl.when(k == at)
            def _():
                halo_wait(group, side)

    def lon_conv(layer, ks, first_block, number):
        first = first_block * REACH
        dilation = lon_dilation[layer]
        taps = []
        for tap in range(TAPS):
            for g in range(GROUPS):
                pieces = []
                for k in ks:
                    start = wide_col(k) + (tap - HALF) * dilation
                    piece = wide[layer][g, pl.ds(first, number), pl.ds(start, STRIP), :]
                    pieces.append(piece.astype(bf16).reshape(number * STRIP, CG))
                taps.append(jnp.concatenate(pieces, 0))
        total = jnp.dot(
            jnp.concatenate(taps, 1), bank[1, layer], preferred_element_type=f32
        )
        values = []
        for at, k in enumerate(ks):
            for part in range(number // REACH):
                mask = wet[first_block + part, pl.ds(first_col(k), STRIP), :]
                for r in range(REACH):
                    line = part * REACH + r
                    old = state[k, first + line].astype(f32)
                    row = (at * number + line) * STRIP
                    piece = total[row : row + STRIP] * mask[:, r : r + 1]
                    values.append((old + piece).astype(bf16))
        return values

    def early(k):
        edge_copy(k).wait_recv()

        @pl.when(has_far_to)
        def _():
            far_copy(k).start()

        own_copy(2, k).wait()
        own_copy(3, k).wait()
        for b in (1, 2, 3):
            put(k, REACH + place[b], state[k, block(b)], mix_gain[0:1])
        raw_rows(near_copy, has_far_to, near, near_row, k)

    def raw_rows(copy, there, ref, row, k):
        @pl.when(there)
        def _():
            copy(k).wait_recv()
            put(k, row, ref[k], mix_gain[0:1])

        @pl.when(jnp.logical_not(there))
        def _():
            normed[k, pl.ds(row, REACH)] = jnp.zeros((REACH, STRIP, C), bf16)

    def outer_lat(k):
        raw_rows(far_copy, has_near_to, far, far_row, k)
        lat_conv((k,), 1)

    def lon_first(k, first, number):
        values = lon_conv(0, (k,), first, number * REACH)
        for at in range(number):
            b = first + at
            part = jnp.stack(values[at * REACH : (at + 1) * REACH], 0)
            state[k, block(b)] = part
            put(k, REACH + place[b], part, mix_gain[1:2])

    def outer_lon(k):
        halo_check(1, k)
        lon_first(k, 3, 1)

        @pl.when(has_near_to)
        def _():
            near2_copy(k).start()

    def finish(ks, first_block, number):
        first = first_block * REACH
        new = jnp.concatenate(lon_conv(1, ks, first_block, number), 0).astype(f32)
        lifted = scaled(new, mlp_gain[...]).astype(bf16)
        half = 0.5 * jnp.dot(lifted, v_in[...], preferred_element_type=f32)
        hidden = (half + half * jnp.tanh(half)).astype(bf16)
        update = jnp.dot(hidden, v_out[...], preferred_element_type=f32)
        result = (new + update).astype(bf16).reshape(len(ks) * number, STRIP, C)
        for at, k in enumerate(ks):
            part = result[at * number : (at + 1) * number]
            if number == REACH:
                state[k, pl.ds(first, number)] = part
                continue
            for row, here in ((other, part[:REACH]), (member, part[REACH:])):
                out[member, pl.ds(REACH * row, REACH), pl.ds(first_col(k), STRIP)] = here

    def halo_rows(copy, there, ref, row, k):
        @pl.when(there)
        def _():
            copy(k).wait_recv()
            normed[k, pl.ds(row, REACH)] = ref[k]

        @pl.when(jnp.logical_not(there))
        def _():
            normed[k, pl.ds(row, REACH)] = jnp.zeros((REACH, STRIP, C), bf16)

    early(0)

    def step(k, carry):
        @pl.when(k + 2 < strips)
        def _():
            early(k + 1)

        @pl.when(k + 1 == strips)
        def _():
            early(k)

        before = jnp.where(k + 1 == strips, k - 1, k)

        @pl.when(jnp.logical_or(k + 2 < strips, k + 1 == strips))
        def _():
            outer_lat(before)

        @pl.when(jnp.logical_and(k >= 1, jnp.logical_or(k + 2 < strips, k + 1 == strips)))
        def _():
            outer_lon(before - 1)

        @pl.when(k < strips)
        def _():
            rest_copy(k).wait_recv()
            put(k, REACH + place[0], state[k, block(0)], mix_gain[0:1])
            lat_conv((k,), 0)

        @pl.when(jnp.logical_and(k >= 1, k <= strips))
        def _():
            j = k - 1
            halo_check(0, j)

            @pl.when(has_far_to)
            def _():
                far_copy(j).wait_send()

            lon_first(j, 0, 3)

            @pl.when(has_far_to)
            def _():
                far2_copy(j).start()

        edge = (k >= strips + 2).astype(jnp.int32)
        at = k - edge * (strips + 2)

        @pl.when(jnp.logical_and(edge == 1, at < strips))
        def _():
            halo_rows(near2_copy, has_far_to, near2, near_row, at)

        j = k - 1 - edge * (strips + 1)

        @pl.when(jnp.logical_and(j >= 0, j < strips))
        def _():
            lat_conv((j,), 2 + edge)

        i = k - 2 - edge * (strips + 1)

        @pl.when(jnp.logical_and(i >= 0, i < strips))
        def _():
            halo_check(2 + edge, i)
            finish((i,), edge, REACH)
            back_copy(edge, i).start()

        @pl.when(jnp.logical_and(edge == 1, at < strips))
        def _():
            halo_rows(far2_copy, has_near_to, far2, far_row, at)
            lat_conv((at,), 4)

        @pl.when(k == strips - 1)
        def _():
            outer_lat(k)

        @pl.when(jnp.logical_or(k == strips, k == strips + 1))
        def _():
            outer_lon(k - 2)

        return carry

    lax.fori_loop(0, 2 * strips + 3, step, 0)

    for side in range(2):
        halo_wait(4, side)

    def keep_step(pair, carry):
        ks = (2 * pair, 2 * pair + 1)
        finish(ks, 2, 2 * REACH)
        return carry

    lax.fori_loop(0, strips // 2, keep_step, 0)

    for group in range(len(GROUPED)):
        for side in range(2):
            halo_copy(group, side).wait_send()
    for b in (0, 1):
        sea_copy(b).wait_send()
    for k in range(strips):
        edge_copy(k).wait_send()
        rest_copy(k).wait_send()

        @pl.when(has_near_to)
        def _():
            near_copy(k).wait_send()
            near2_copy(k).wait_send()

        @pl.when(has_far_to)
        def _():
            far2_copy(k).wait_send()

        back_copy(0, k).wait()
        back_copy(1, k).wait()


def on_device(
    fields,
    mix_gain,
    lat_weight,
    lon_weight,
    mlp_gain,
    w_in,
    w_out,
    lat_dilation,
    lon_dilation,
    ocean,
):
    cols = fields.shape[2]
    strips = cols // STRIP
    count = lax.axis_size("lat")
    width = -(-cols // 128) * 128
    vmem = pl.BlockSpec(memory_space=pltpu.VMEM)
    hbm = pl.BlockSpec(memory_space=pl.ANY)
    held = pltpu.VMEM((strips, ROWS, STRIP, C), bf16)
    halo = pltpu.VMEM((strips, REACH, STRIP, C), bf16)
    wide = pltpu.VMEM((GROUPS, ROWS, cols + 2 * STRIP, CG), f32)
    ends = pltpu.VMEM((LAYERS, 2, ROWS, STRIP, C), bf16)
    dma = pltpu.SemaphoreType.DMA
    cells = 2 * fields.shape[1] * cols
    return pl.pallas_call(
        functools.partial(kernel, count, strips),
        in_specs=[hbm] * 10,
        out_specs=vmem,
        out_shape=pltpu.VMEM(fields.shape, bf16),
        scratch_shapes=[
            held,
            halo,
            halo,
            halo,
            halo,
            pltpu.VMEM((strips, ROWS + 2 * REACH, STRIP, C), bf16),
            wide,
            wide,
            ends,
            ends,
            pltpu.VMEM((2, LAYERS, TAPS, GROUPS, CG, CG), bf16),
            pltpu.VMEM((2, LAYERS, TAPS * C, C), bf16),
            pltpu.VMEM((C, HIDDEN), bf16),
            pltpu.VMEM((HIDDEN, C), bf16),
            pltpu.VMEM((BLOCKS, REACH, cols), jnp.int32),
            pltpu.VMEM((128, width), f32),
            pltpu.VMEM((BLOCKS, width, 128), f32),
            pltpu.SMEM((LAYERS,), jnp.int32),
            pltpu.SMEM((LAYERS,), jnp.int32),
            pltpu.VMEM((LAYERS, C), f32),
            pltpu.VMEM((1, C), f32),
            dma((8, strips)),
            dma((8, strips)),
            dma((len(GROUPED), 2)),
            dma((len(GROUPED), 2)),
            dma((2,)),
            dma((2,)),
            dma((10,)),
            dma((2, strips)),
        ],
        compiler_params=pltpu.CompilerParams(
            collective_id=0, has_side_effects=True, vmem_limit_bytes=VMEM_LIMIT
        ),
        cost_estimate=pl.CostEstimate(
            flops=2 * cells * (2 * LAYERS * TAPS * C * C + 2 * C * HIDDEN),
            bytes_accessed=4 * cells * C,
            transcendentals=cells * HIDDEN,
        ),
    )(
        lat_dilation,
        lon_dilation,
        fields,
        ocean,
        mix_gain,
        mlp_gain.reshape(1, C),
        lat_weight,
        lon_weight,
        w_in,
        w_out,
    )


def solution(mesh):
    return jax.shard_map(
        on_device,
        mesh=mesh,
        in_specs=(
            P("grp", "lat", "lon", None),
            P(),
            P(),
            P(),
            P(),
            P(),
            P(),
            P(),
            P(),
            P(("grp", "lat"), "lon"),
        ),
        out_specs=P("grp", "lat", "lon", None),
        check_vma=False,
    )
```
